128 devices in a mesh: frame: 8 (over x_lo, y), row: 16 (over x_hi, z, core).
Axes of the slice: x: 4 (x_hi: 2, x_lo: 2; x = x_hi * 2 + x_lo), y: 4, z: 4, core: 2. Of those that a mesh axis runs over, the one named last changes fastest.
Arguments:
- features: bfloat16 [16, 32, 128, 128], P('frame', 'row'), may hold values from -6 to 6
- row_shift: int32 [16, 8], replicated, may hold values from -2 to 2, as said below
- lidar_points: int32 [16, 3, 8192], P('frame', None, 'row'), may hold values from 0 to 127, as said below
- conv_first: bfloat16 [8, 8, 3, 3, 3], replicated, may hold values from -0.4375 to 0.4375
- conv_last: bfloat16 [1, 8, 3, 3, 3], replicated, may hold values from -0.4375 to 0.4375
Outputs:
- occupancy: bfloat16 [16, 96, 32, 128], P('frame', None, 'row')
- logit_grad: float32 [16, 96, 32, 128], P('frame', None, 'row')
The draws below stay inside these ranges and needn't reach their ends.
Inputs may be any that keep to these rules, and one draw needn't show every extreme that they name: `row_shift`: some entry equals 2 and some equals -2. `lidar_points`: component 0 is a row below 32, 1 a column below 128, 2 a depth bin below 96. Of the 512 points of one frame held by one index of row, at most 96 lie in any one panel of 2 rows starting at a multiple of 2; in every frame one such panel receives exactly 96 from every holder.
All inputs are finite; a program needn't handle non-finite values.
Results may differ from the reference program's by a relative error of at most 0.003.
Values may be sent and summed in bfloat16 or wider, within the bound.
A program may use at most 128 MiB of HBM per device.

```python
import math
import jax
import jax.numpy as jnp
from jax import lax

C = 128
G = 8
D = 96
HIST = 8
ROW_REACH = 2
W = 128
ROWS_DEV = 2
PTS_DEV = 512
FRAMES = 16
H = 32
PTS = 8192
CAP = 96


def draw_row_shift(key, part):
    key_values, key_position = jax.random.split(jax.random.fold_in(key, 11), 2)
    offsets = jax.random.randint(key_values, (FRAMES * HIST,), -ROW_REACH, ROW_REACH + 1)
    position = jax.random.randint(key_position, (), 0, FRAMES * HIST - 1)
    offsets = offsets.at[position].set(ROW_REACH).at[position + 1].set(-ROW_REACH)
    return offsets.reshape(FRAMES, HIST).astype(jnp.int32)


def draw_lidar_points(key, part):
    row_devices = H // ROWS_DEV
    keys = jax.random.split(jax.random.fold_in(key, 23), 5)
    places = jnp.arange(PTS_DEV, dtype=jnp.int32)
    remainder = PTS_DEV - CAP
    base_owner = jnp.where(places < CAP, 0, 1 + (places - CAP) * (row_devices - 1) // remainder)
    rotation = jax.random.randint(keys[0], (FRAMES,), 0, row_devices)
    rotation = rotation.at[0].set(0).at[FRAMES - 1].set(row_devices - 1)
    owner_rank = (base_owner[None, None, :] + rotation[:, None, None]) % row_devices
    owner_rank = jnp.broadcast_to(owner_rank, (FRAMES, row_devices, PTS_DEV))
    local_row = jax.random.randint(keys[1], (FRAMES, row_devices, PTS_DEV), 0, ROWS_DEV)
    local_row = jnp.where(places == 0, ROWS_DEV - 1, jnp.where(places == 1, 0, local_row))
    column = jax.random.randint(keys[2], (FRAMES, row_devices, PTS_DEV), 0, W)
    column = jnp.where(places == 0, W - 1, column)
    depth_bin = jax.random.randint(keys[3], (FRAMES, row_devices, PTS_DEV), 0, D)
    stacked = jnp.stack([owner_rank * ROWS_DEV + local_row, column, depth_bin], 0)
    block_keys = jax.random.split(keys[4], FRAMES * row_devices)
    shuffles = jax.vmap(lambda block_key: jax.random.permutation(block_key, PTS_DEV))(block_keys)
    shuffles = shuffles.reshape(FRAMES, row_devices, PTS_DEV)
    shuffled = jnp.take_along_axis(stacked, jnp.broadcast_to(shuffles[None], stacked.shape), axis=3)
    return jnp.transpose(shuffled, (1, 0, 2, 3)).reshape(FRAMES, 3, row_devices * PTS_DEV).astype(jnp.int32)


def block_levels(key, shape, cuts, low, top_value):
    factor_of = 1.0
    for dim, shards_of in cuts:
        steps = jax.random.uniform(jax.random.fold_in(jax.random.fold_in(key, 6), dim), (shards_of,), jnp.float32, low / len(cuts), top_value / len(cuts))
        factor_of = factor_of * jnp.repeat(jnp.exp(steps), shape[dim] // shards_of).reshape((-1,) + (1,) * (len(shape) - 1 - dim))
    return factor_of


def gaussian(own_key, dims, deviation, reach, cuts=(), kind=jnp.bfloat16):
    level = block_levels(own_key, dims, cuts, -0.22, 0.18) if cuts else 1.0
    entries = jax.random.normal(own_key, dims, jnp.float32) * deviation * level
    return jnp.minimum(jnp.maximum(entries, -reach), reach).astype(kind)


def setup_inputs(seed: int = 0) -> dict:
    arg_keys = jax.random.split(jax.random.key(seed), 6)
    features = gaussian(arg_keys[0], (FRAMES, H, W, C), 1.0, 6.0, ((0, 8), (1, 16)))
    row_shift = draw_row_shift(jax.random.fold_in(arg_keys[5], 71), 0)
    lidar_points = draw_lidar_points(jax.random.fold_in(arg_keys[5], 71), 0)
    conv_first = gaussian(arg_keys[3], (G, G, 3, 3, 3), (27 * G) ** -0.5, 0.4375)
    conv_last = gaussian(arg_keys[4], (1, G, 3, 3, 3), (27 * G) ** -0.5, 0.4375)
    return {"features": features, "row_shift": row_shift, "lidar_points": lidar_points, "conv_first": conv_first, "conv_last": conv_last}


def conv_cube(volume, weights):
    return lax.conv_general_dilated(volume, weights, (1, 1, 1), ((1, 1), (1, 1), (1, 1)), dimension_numbers=('NCDHW', 'OIDHW', 'NCDHW'))

def reference(features, row_shift, lidar_points, conv_first, conv_last):
    group_width = C // G
    score_scale = 1.0 / math.sqrt(HIST * group_width)
    padded = jnp.pad(features, ((HIST, 0), (ROW_REACH, ROW_REACH), (D, 0), (0, 0)))
    depth_ids = jnp.arange(D, dtype=jnp.int32)
    zero_index = jnp.zeros((), jnp.int32)

    def frame_logits(frame_id):
        queries = features[frame_id].astype(jnp.float32).reshape(H, W, G, group_width)
        totals = jnp.zeros((D, G, H, W), jnp.float32)
        for lag_step in range(1, HIST + 1):
            offset = row_shift[frame_id, lag_step - 1]
            frame_start = (frame_id + (HIST - lag_step)).astype(jnp.int32)
            row_start = (offset + ROW_REACH).astype(jnp.int32)
            source = lax.dynamic_slice(padded, (frame_start, row_start, zero_index, zero_index), (1, H, D + W, C))[0].astype(jnp.float32)

            def depth_scores(depth_id):
                column_start = (D - depth_id * lag_step // HIST).astype(jnp.int32)
                key_block = lax.dynamic_slice(source, (zero_index, column_start, zero_index), (H, W, C)).reshape(H, W, G, group_width)
                return jnp.transpose(lax.optimization_barrier(jnp.sum(key_block * queries, axis=-1)), (2, 0, 1))
            totals = totals + lax.map(depth_scores, depth_ids)
        cost_volume = lax.optimization_barrier((totals * score_scale).astype(jnp.bfloat16))
        cost_volume = jnp.transpose(cost_volume, (1, 0, 2, 3))
        first_layer = conv_cube(cost_volume.astype(jnp.float32)[None], conv_first.astype(jnp.float32))
        hidden = lax.optimization_barrier(jnp.maximum(first_layer, 0.0).astype(jnp.bfloat16))
        return conv_cube(hidden.astype(jnp.float32), conv_last.astype(jnp.float32))[0, 0]
    logits = lax.map(frame_logits, jnp.arange(FRAMES, dtype=jnp.int32))
    occupancy = jax.nn.sigmoid(logits).astype(jnp.bfloat16)
    frame_ids = jnp.broadcast_to(jnp.arange(FRAMES, dtype=jnp.int32)[:, None], (FRAMES, PTS))
    row_hit = lidar_points[:, 0, :]
    column_hit = lidar_points[:, 1, :]
    depth_hit = lidar_points[:, 2, :]
    hit_counts = jnp.zeros((FRAMES, H, W), jnp.float32).at[frame_ids, row_hit, column_hit].add(1.0)
    target_counts = jnp.zeros((FRAMES, D, H, W), jnp.float32).at[frame_ids, depth_hit, row_hit, column_hit].add(1.0)
    logit_grad = hit_counts[:, None] * jax.nn.sigmoid(logits) - target_counts
    return (occupancy, logit_grad)
```

```python
import functools
import math

import jax
import jax.numpy as jnp
from jax import lax
from jax.experimental import pallas as pl
from jax.experimental.pallas import tpu as pltpu

G = 8
D = 96
HIST = 8
W = 128
TILES = 4
STEP = D // TILES
F32, BF16, I32 = jnp.float32, jnp.bfloat16, jnp.int32
NT = (((1,), (1,)), ((), ()))
SCALE = 1.0 / math.sqrt(HIST * 16)


def iota(shape, dim):
    return lax.broadcasted_iota(I32, shape, dim)


def build_tables(v_ref, t1, t2, idx):
    m = iota((32, 256), 1) % 32
    li = iota((32, 256), 0)
    masks = [(li == m + a) & (m < STEP + 2) for a in range(3)]

    def first(b, c):
        for e in range(3):
            for i in range(G):
                block = jnp.zeros((32, 256), F32)
                for a in range(3):
                    row = v_ref[pl.ds((i * 3 + a) * 9 + e + 3 * b, 1), :]
                    block = jnp.where(masks[a], row, block)
                at = (e * G + i) * 32
                t1[b, at : at + 32, :] = block.astype(BF16)
        return c

    lax.fori_loop(0, 3, first, 0)
    rows2 = [(m == li + a) & (li < STEP) for a in range(3)]

    def last(b, c):
        for e in range(3):
            block = jnp.zeros((32, 256), F32)
            for a in range(3):
                row = v_ref[pl.ds(216 + a * 9 + e + 3 * b, 1), :]
                block = jnp.where(rows2[a], row, block)
            t2[b, e * 32 : e * 32 + 32, :] = block.astype(BF16)
        return c

    lax.fori_loop(0, 3, last, 0)

    def lag(k0, c):
        lane = iota((W, W), 1)
        w = iota((W, W), 0)
        for gq in range(4):
            tile = (lane // 32 - gq + 4) % 4
            low = lane % 32
            d = STEP * tile - 2 + low
            ok = (low < STEP + 4) & (d >= 0) & (d < D)
            s = jnp.where(ok, (d * (k0 + 1)) >> 3, 1000)
            idx[k0, gq] = w - s
        return c

    lax.fori_loop(0, HIST, lag, 0)


def compute_kernel(pos, shift, win, pts, v_ref, occ, grad, t1, t2, idx, qm, kbuf, mres, acc, pad, x3, hid, tgt):
    slot = pl.program_id(0)
    frame, row = pos[0], pos[1]
    t = 2 * frame + slot

    @pl.when(slot == 0)
    def _():
        build_tables(v_ref, t1, t2, idx)

    lane = iota((W, W), 1)

    tgt[...] = jnp.zeros_like(tgt)

    def points(src, c):
        p = pts[src, slot].astype(F32)
        local = p[0:1] - (2 * row).astype(F32)
        inside = (local >= 0) & (local < 2)
        code = jnp.where(inside, local * W + p[1:2], -1.0).astype(I32)
        dep = p[2:3].astype(I32)
        n = p.shape[1]
        bins = iota((104, n), 0)
        left = jnp.where((bins == dep) | (bins >= D), 1.0, 0.0).astype(BF16)
        right = jnp.where(iota((256, n), 0) == code, 1.0, 0.0).astype(BF16)
        tgt[...] += lax.dot_general(left, right, NT, preferred_element_type=F32)
        return c

    lax.fori_loop(0, pts.shape[0], points, 0)

    for s in range(2 * TILES):
        pad[s, 0:8, :] = jnp.zeros((8, W), F32)
        pad[s, 136:144, :] = jnp.zeros((8, W), F32)

    def cost_row(ro, c):
        rr = ro + 2
        q = win[rr // 2, 0, slot, rr % 2]
        for g in range(G):
            qm[g * W : (g + 1) * W, :] = jnp.where(lane // 16 == g, q, jnp.zeros_like(q))
        acc[...] = jnp.zeros_like(acc)

        def lags(kp, c2):
            for kk in range(2):
                k = 2 * kp + 1 + kk
                j = (k - slot + 1) // 2
                fi = slot - k + 2 * j
                rs = rr + shift[t, k - 1]
                src = 2 * row - 4 + rs
                ok = (t - k >= 0) & (src >= 0) & (src < 32)
                key = win[rs // 2, j, fi, rs % 2]
                kbuf[kk * W : (kk + 1) * W, :] = jnp.where(ok, key, jnp.zeros_like(key))
            mres[...] = lax.dot_general(qm[...], kbuf[...], NT, preferred_element_type=F32)
            for gq in range(4):
                for kk in range(2):
                    raw = idx[2 * kp + kk, gq]
                    at = raw & 127
                    ok = raw >= 0
                    for g in (gq, gq + 4):
                        x = mres[g * W : (g + 1) * W, kk * W : (kk + 1) * W]
                        y = jnp.take_along_axis(x, at, axis=1, mode="promise_in_bounds")
                        acc[g] += jnp.where(ok, y, 0.0)
            return c2

        lax.fori_loop(0, HIST // 2, lags, 0)
        src = 2 * row - 2 + ro
        live = (src >= 0) & (src < 32)
        scale = jnp.where(live, SCALE, 0.0)
        for j in range(TILES):
            for h in range(2):
                x = acc[4 * h]
                for gq in range(4):
                    x = jnp.where(lane // 32 == (j + gq) % 4, acc[4 * h + gq], x)
                x = jnp.where(live, x * SCALE, 0.0)
                if j:
                    x = pltpu.roll(x, W - 32 * j, 1)
                s = 2 * j + h
                pad[s, 8 : 8 + W, :] = x
                for e in range(3):
                    x3[j, ro, :, e * 256 + h * W : e * 256 + (h + 1) * W] = pad[
                        s, 7 + e : 7 + e + W, :
                    ].astype(BF16)
        return c

    lax.fori_loop(0, 6, cost_row, 0)

    def tile(j, c):
        total = jnp.dot(x3[j, 0:4].reshape(4 * W, 768), t1[0], preferred_element_type=F32)
        for b in (1, 2):
            total += jnp.dot(x3[j, b : b + 4].reshape(4 * W, 768), t1[b], preferred_element_type=F32)
        d = STEP * j - 1 + iota((W, 256), 1) % 32
        inside = (d >= 0) & (d < D)
        for h in range(4):
            src = 2 * row - 1 + h
            ok = inside & ((src >= 0) & (src < 32))
            hid[h] = jnp.where(ok, jnp.maximum(total[h * W : (h + 1) * W], 0.0), 0.0).astype(BF16)
        out = jnp.zeros((96, 256), F32)
        for b in range(3):
            out += lax.dot_general(t2[b], hid[b : b + 2].reshape(256, 256), NT, preferred_element_type=F32)
        for r in range(2):
            cut = out[:, r * W : (r + 1) * W]
            wl = iota((STEP, W), 1)
            logits = (
                cut[32 : 32 + STEP]
                + jnp.where(wl == 0, 0.0, pltpu.roll(cut[0:STEP], 1, 1))
                + jnp.where(wl == W - 1, 0.0, pltpu.roll(cut[64 : 64 + STEP], W - 1, 1))
            )
            sig = jax.nn.sigmoid(logits)
            ds = pl.ds(j * STEP, STEP)
            occ[0, ds, r, :] = sig.astype(BF16)
            hits = tgt[D : D + 1, r * W : (r + 1) * W]
            grad[0, ds, r, :] = hits * sig - tgt[pl.ds(pl.multiple_of(j * STEP, 8), STEP), r * W : (r + 1) * W]
        return c

    lax.fori_loop(0, TILES, tile, 0)


def local_compute(pos, shift, win, pts, v):
    vmem = pl.BlockSpec(memory_space=pltpu.VMEM)
    smem = pl.BlockSpec(memory_space=pltpu.SMEM)
    block = pl.BlockSpec((1, D, 2, W), lambda s: (s, 0, 0, 0))
    return pl.pallas_call(
        compute_kernel,
        grid=(2,),
        out_shape=(
            jax.ShapeDtypeStruct((2, D, 2, W), BF16),
            jax.ShapeDtypeStruct((2, D, 2, W), F32),
        ),
        in_specs=[smem, smem, vmem, vmem, vmem],
        out_specs=(block, block),
        scratch_shapes=[
            pltpu.VMEM((3, 768, 256), BF16),
            pltpu.VMEM((3, 96, 256), BF16),
            pltpu.VMEM((HIST, 4, W, W), I32),
            pltpu.VMEM((G * W, W), BF16),
            pltpu.VMEM((2 * W, W), BF16),
            pltpu.VMEM((G * W, 2 * W), F32),
            pltpu.VMEM((G, W, W), F32),
            pltpu.VMEM((2 * TILES, 144, W), F32),
            pltpu.VMEM((TILES, 6, W, 768), BF16),
            pltpu.VMEM((4, W, 256), BF16),
            pltpu.VMEM((104, 256), F32),
        ],
        compiler_params=pltpu.CompilerParams(vmem_limit_bytes=60000 * 1024),
        name="local_compute",
    )(pos, shift, win, pts, v)


def weight_rows(conv_first, conv_last):
    both = jnp.concatenate(
        [conv_first.reshape(G, 216).T, conv_last.reshape(G, 27).T, jnp.zeros((5, G), BF16)], 0
    )
    return jnp.repeat(both.astype(F32), 32, axis=1)


MESH = pl.DeviceIdType.MESH
REACH = 4
ORDER = (0, 1, 4, 3, 2)


def gather_kernel(feat, pts, win, allpts, send, recv, relay_send, psend, precv, own):
    f = lax.axis_index("frame")
    r = lax.axis_index("row")
    frames = lax.axis_size("frame")
    rows = lax.axis_size("row")
    core = r % 2
    barrier = pltpu.get_barrier_semaphore()

    def greet(there_f, there_r):
        pl.semaphore_signal(
            barrier, inc=1, device_id={"frame": there_f, "row": there_r}, device_id_type=MESH
        )

    for off in range(1, rows):
        greet(f, (r + off) % rows)
    for j in range(1, REACH + 1):
        pl.when(f + j < frames)(lambda j=j: greet(f + j, r))
        pl.when(f - j >= 0)(lambda j=j: greet(f - j, r))
    later = jnp.minimum(frames - 1 - f, REACH)
    earlier = jnp.minimum(f, REACH)
    pl.semaphore_wait(barrier, rows - 1 + later + earlier)

    def frame_copy(j, there):
        return pltpu.make_async_remote_copy(
            src_ref=feat,
            dst_ref=win.at[2, j],
            send_sem=send.at[0, j],
            recv_sem=recv.at[2, j],
            device_id={"frame": there, "row": r},
            device_id_type=MESH,
        )

    def row_copy(lane, j, q, there, src=None):
        return pltpu.make_async_remote_copy(
            src_ref=(feat if j == 0 else win.at[2, j]) if src is None else src,
            dst_ref=win.at[q, j],
            send_sem=send.at[lane, j] if src is None else relay_send.at[j],
            recv_sem=recv.at[q, j],
            device_id={"frame": f, "row": there},
            device_id_type=MESH,
        )

    def point_copy(off):
        there = (r + off) % rows
        return pltpu.make_async_remote_copy(
            src_ref=pts,
            dst_ref=allpts.at[r],
            send_sem=psend.at[off],
            recv_sem=precv.at[r],
            device_id={"frame": f, "row": there},
            device_id_type=MESH,
        )

    def point_arrival(off):
        there = (r + off) % rows
        return pltpu.make_async_remote_copy(
            src_ref=pts,
            dst_ref=allpts.at[there],
            send_sem=psend.at[off],
            recv_sem=precv.at[there],
            device_id={"frame": f, "row": there},
            device_id_type=MESH,
        )

    routes = {0: ((1, 1, 1), (2, 0, 2), (3, 3, -1)), 1: ((1, 3, -1), (2, 1, 1), (3, 4, -2))}
    relays = {0: (1, 0, 1), 1: (3, 4, -1)}

    def inside(there):
        return (there >= 0) & (there < rows)

    def row_sends(j, act):
        for c in range(2):
            for lane, q, off in routes[c]:
                ok = (core == c) & inside(r + off) & (f >= j)
                pl.when(ok)(lambda lane=lane, q=q, off=off: act(row_copy(lane, j, q, r + off)))

    def relay(j, act, wait_first):
        for c in range(2):
            here, q, off = relays[c]
            source = r - 1 if c == 0 else r + 1
            ok = (core == c) & inside(source) & (f >= j)

            def body(here=here, q=q, off=off):
                if wait_first:
                    row_copy(1, j, here, r + off).wait_recv()
                act(row_copy(0, j, q, r + off, src=win.at[here, j]))

            pl.when(ok)(body)

    def start(copy):
        copy.start()

    mine = pltpu.make_async_copy(feat, win.at[2, 0], own.at[0])
    mine_pts = pltpu.make_async_copy(pts, allpts.at[r], own.at[1])
    mine.start()
    mine_pts.start()
    for j in (1, 4, 3, 2):
        pl.when(f + j < frames)(lambda j=j: frame_copy(j, f + j).start())
    row_sends(0, start)
    for off in range(1, rows):
        point_copy(off).start()
    for n, j in enumerate(ORDER):
        if j:
            pl.when(f >= j)(lambda j=j: frame_copy(j, f).wait_recv())
            row_sends(j, start)
        if n:
            relay(ORDER[n - 1], start, True)
    relay(ORDER[-1], start, True)

    for j in ORDER:
        for c, slots in ((0, ((0, -2), (3, 1), (4, 2))), (1, ((0, -2), (1, -1), (4, 2)))):
            for q, off in slots:
                ok = (core == c) & inside(r + off) & (f >= j)
                pl.when(ok)(lambda q=q, j=j: row_copy(1, j, q, r).wait_recv())
    for off in range(1, rows):
        point_arrival(off).wait_recv()
    for j in range(1, REACH + 1):
        pl.when(f + j < frames)(lambda j=j: frame_copy(j, f + j).wait_send())
    for j in ORDER:
        row_sends(j, lambda copy: copy.wait_send())
        relay(j, lambda copy: copy.wait_send(), False)
    for off in range(1, rows):
        point_copy(off).wait_send()
    mine.wait()
    mine_pts.wait()


def gather(features, points):
    frames, rows, cols, chans = features.shape
    count = lax.axis_size("row")
    vmem = pl.BlockSpec(memory_space=pltpu.VMEM)
    hbm = pl.BlockSpec(memory_space=pl.ANY)
    dma = pltpu.SemaphoreType.DMA
    return pl.pallas_call(
        gather_kernel,
        out_shape=(
            jax.ShapeDtypeStruct((5, REACH + 1) + features.shape, features.dtype),
            jax.ShapeDtypeStruct((count,) + points.shape, points.dtype),
        ),
        in_specs=[vmem, vmem],
        out_specs=(hbm, hbm),
        scratch_shapes=[
            dma((4, REACH + 1)),
            dma((5, REACH + 1)),
            dma((REACH + 1,)),
            dma((count,)),
            dma((count,)),
            dma((2,)),
        ],
        compiler_params=pltpu.CompilerParams(collective_id=0, has_side_effects=True),
        name="gather_window",
    )(features, points)


def shards(features, row_shift, lidar_points, conv_first, conv_last):
    pos = jnp.stack([lax.axis_index("frame"), lax.axis_index("row")]).astype(I32)
    win, pts = gather(features, lidar_points.astype(BF16))
    return local_compute(pos, row_shift, win, pts, weight_rows(conv_first, conv_last))


def solution(mesh):
    P = jax.sharding.PartitionSpec
    out = P("frame", None, "row", None)
    return jax.shard_map(
        shards,
        mesh=mesh,
        in_specs=(P("frame", "row", None, None), P(), P("frame", None, "row"), P(), P()),
        out_specs=(out, out),
        check_vma=False,
    )
```

```python
import functools
import math

import jax
import jax.numpy as jnp
from jax import lax
from jax.experimental import pallas as pl
from jax.experimental.pallas import tpu as pltpu

G = 8
D = 96
HIST = 8
W = 128
TILES = 4
STEP = D // TILES
F32, BF16, I32 = jnp.float32, jnp.bfloat16, jnp.int32
NT = (((1,), (1,)), ((), ()))
PAIRS = ((8, 2, 6), (7, 1, 6), (6, 3, 5), (5, 4, 4))
SCALE = 1.0 / math.sqrt(HIST * 16)


def iota(shape, dim):
    return lax.broadcasted_iota(I32, shape, dim)


def build_tables(v_ref, t1, t2, band, pick, back):
    m = iota((32, 256), 1) % 32
    li = iota((32, 256), 0)
    masks = [(li == m + a) & (m < STEP + 2) for a in range(3)]

    def first(b, c):
        for e in range(3):
            for i in range(G):
                block = jnp.zeros((32, 256), F32)
                for a in range(3):
                    row = v_ref[pl.ds((i * 3 + a) * 9 + e + 3 * b, 1), :]
                    block = jnp.where(masks[a], row, block)
                at = (e * G + i) * 32
                t1[0, b, at : at + 32, :] = block.astype(BF16)
        return c

    lax.fori_loop(0, 3, first, 0)
    rows2 = [(m == li + a) & (li < STEP) for a in range(3)]

    def last(b, c):
        for e in range(3):
            block = jnp.zeros((32, 256), F32)
            for a in range(3):
                row = v_ref[pl.ds(216 + a * 9 + e + 3 * b, 1), :]
                block = jnp.where(rows2[a], row, block)
            t2[b, e * 32 : e * 32 + 32, :] = block.astype(BF16)
        return c

    lax.fori_loop(0, 3, last, 0)

    lane = iota((W, W), 1)
    w = iota((W, W), 0)
    for p, (ka, kb, turn) in enumerate(PAIRS):
        for n, (k, base) in enumerate(((ka, 0), (kb, 16 * turn))):
            s = (lane + w + 1 - base) & (W - 1)
            ok = (s < 12 * k) & (s <= w)
            band[p, n] = jnp.where(ok, 1.0, 0.0).astype(BF16)
    for gq in range(4):
        low = lane % 32
        d = STEP * ((lane // 32 - gq + 4) % 4) - 2 + low
        real = (low < STEP + 4) & (d >= 0) & (d < D)
        for p, (ka, kb, turn) in enumerate(PAIRS):
            hit = (w == (((d * ka) >> 3) + W - 1) % W) | (w == (((d * kb) >> 3) + 16 * turn - 1) % W)
            pick[gq, p * W : (p + 1) * W, :] = jnp.where(hit & real, 1.0, 0.0).astype(BF16)
    back[...] = jnp.where(lane + w == W - 1, 1.0, 0.0).astype(BF16)

    def turned(b, c):
        for j in range(1, TILES):
            for e in range(3):
                for h in range(2):
                    for q in range(4):
                        at = e * 256 + h * W
                        t1[j, b, at + q * 32 : at + q * 32 + 32, :] = t1[
                            0, b, at + ((q - j) % 4) * 32 : at + ((q - j) % 4) * 32 + 32, :
                        ]
        return c

    lax.fori_loop(0, 3, turned, 0)


def compute_kernel(
    pos, shift, win, tgt, v_ref, occ, grad, t1, t2, band, pick, back, qm, kbuf, skew, pad, x3, hid
):
    slot = pl.program_id(0)
    frame, row = pos[0], pos[1]
    t = 2 * frame + slot

    @pl.when(slot == 0)
    def _():
        build_tables(v_ref, t1, t2, band, pick, back)

    lane = iota((W, W), 1)
    for s in range(2 * TILES):
        pad[s, 0:8, :] = jnp.zeros((8, W), F32)
        pad[s, 136:144, :] = jnp.zeros((8, W), F32)

    def cost_row(ro, c):
        rr = ro + 2
        q = win[rr // 2, 0, slot, rr % 2]
        for g in range(G):
            qm[g * W : (g + 1) * W, :] = jnp.where(lane // 16 == g, q, jnp.zeros_like(q))
        for p, (ka, kb, turn) in enumerate(PAIRS):
            for n, k in enumerate((ka, kb)):
                j = (k - slot + 1) // 2
                fi = slot - k + 2 * j
                rs = rr + shift[t, k - 1]
                src = 2 * row - 4 + rs
                ok = (t - k >= 0) & (src >= 0) & (src < 32)
                key = win[rs // 2, j, fi, rs % 2]
                key = jnp.where(ok, key, jnp.zeros_like(key))
                key = jnp.dot(back[...], key, preferred_element_type=F32).astype(BF16)
                if n:
                    cut = W - 16 * turn
                    kbuf[p, W + 16 * turn : 2 * W, :] = key[0:cut]
                    kbuf[p, W : W + 16 * turn, :] = key[cut:W]
                else:
                    kbuf[p, 0:W, :] = key
        for p in range(4):
            m = lax.dot_general(qm[...], kbuf[p], NT, preferred_element_type=F32)
            for g in range(G):
                rows = m[g * W : (g + 1) * W].astype(BF16)
                both = rows[:, 0:W] * band[p, 0] + rows[:, W : 2 * W] * band[p, 1]
                skew[g * W : (g + 1) * W, p * W : (p + 1) * W] = pltpu.roll(
                    both, 0, 1, stride=1, stride_axis=0
                )
        src = 2 * row - 2 + ro
        live = (src >= 0) & (src < 32)
        for h in range(2):
            picked = [
                jnp.dot(
                    skew[(4 * h + gq) * W : (4 * h + gq + 1) * W, :],
                    pick[gq],
                    preferred_element_type=F32,
                )
                for gq in range(4)
            ]
            for j in range(TILES):
                x = picked[0]
                for gq in range(1, 4):
                    x = jnp.where(lane // 32 == (j + gq) % 4, picked[gq], x)
                s = 2 * j + h
                pad[s, 8 : 8 + W, :] = jnp.where(live, x * SCALE, 0.0)
                for e in range(3):
                    at = e * 256 + h * W
                    x3[j, ro, :, at : at + W] = pad[s, 7 + e : 7 + e + W, :].astype(BF16)
        return c

    lax.fori_loop(0, 6, cost_row, 0)

    def tile(j, c):
        total = jnp.dot(x3[j, 0:4].reshape(4 * W, 768), t1[j, 0], preferred_element_type=F32)
        for b in (1, 2):
            total += jnp.dot(x3[j, b : b + 4].reshape(4 * W, 768), t1[j, b], preferred_element_type=F32)
        d = STEP * j - 1 + iota((W, 256), 1) % 32
        inside = (d >= 0) & (d < D)
        for h in range(4):
            src = 2 * row - 1 + h
            ok = inside & ((src >= 0) & (src < 32))
            hid[h] = jnp.where(ok, jnp.maximum(total[h * W : (h + 1) * W], 0.0), 0.0).astype(BF16)
        out = jnp.zeros((96, 256), F32)
        for b in range(3):
            out += lax.dot_general(t2[b], hid[b : b + 2].reshape(256, 256), NT, preferred_element_type=F32)
        for r in range(2):
            cut = out[:, r * W : (r + 1) * W]
            wl = iota((STEP, W), 1)
            logits = (
                cut[32 : 32 + STEP]
                + jnp.where(wl == 0, 0.0, pltpu.roll(cut[0:STEP], 1, 1))
                + jnp.where(wl == W - 1, 0.0, pltpu.roll(cut[64 : 64 + STEP], W - 1, 1))
            )
            sig = jax.nn.sigmoid(logits)
            ds = pl.ds(j * STEP, STEP)
            occ[0, ds, r, :] = sig.astype(BF16)
            hits = tgt[slot, D : D + 1, r * W : (r + 1) * W]
            spots = tgt[slot, pl.ds(pl.multiple_of(j * STEP, 8), STEP), r * W : (r + 1) * W]
            grad[0, ds, r, :] = hits * sig - spots
        return c

    lax.fori_loop(0, TILES, tile, 0)


def count_points(pts, slot, row, count):
    n = pts.shape[3]
    one = jnp.ones((), BF16)
    zero = jnp.zeros((), BF16)
    bins = iota((104, n), 0)
    spots = iota((256, n), 0).astype(BF16)

    def points(src, total):
        p = pts[src, slot].astype(F32)
        local = p[0:1] - (2 * row).astype(F32)
        inside = (local >= 0) & (local < 2)
        code = jnp.where(inside, local * W + p[1:2], -1.0).astype(BF16)
        dep = p[2:3].astype(BF16)
        left = jnp.where((bins.astype(BF16) == dep) | (bins >= D), one, zero)
        right = jnp.where(spots == code, one, zero)
        return total + lax.dot_general(left, right, NT, preferred_element_type=F32)

    return lax.fori_loop(0, count, points, jnp.zeros((104, 256), F32))


def local_compute(pos, shift, win, tgt, v):
    vmem = pl.BlockSpec(memory_space=pltpu.VMEM)
    smem = pl.BlockSpec(memory_space=pltpu.SMEM)
    block = pl.BlockSpec((1, D, 2, W), lambda s: (s, 0, 0, 0))
    return pl.pallas_call(
        compute_kernel,
        grid=(2,),
        out_shape=(
            jax.ShapeDtypeStruct((2, D, 2, W), BF16),
            jax.ShapeDtypeStruct((2, D, 2, W), F32),
        ),
        in_specs=[smem, smem, vmem, vmem, vmem],
        out_specs=(block, block),
        scratch_shapes=[
            pltpu.VMEM((TILES, 3, 768, 256), BF16),
            pltpu.VMEM((3, 96, 256), BF16),
            pltpu.VMEM((4, 2, W, W), BF16),
            pltpu.VMEM((4, 4 * W, W), BF16),
            pltpu.VMEM((W, W), BF16),
            pltpu.VMEM((G * W, W), BF16),
            pltpu.VMEM((4, 2 * W, W), BF16),
            pltpu.VMEM((G * W, 4 * W), BF16),
            pltpu.VMEM((2 * TILES, 144, W), F32),
            pltpu.VMEM((TILES, 6, W, 768), BF16),
            pltpu.VMEM((4, W, 256), BF16),
        ],
        compiler_params=pltpu.CompilerParams(vmem_limit_bytes=60000 * 1024),
        name="local_compute",
    )(pos, shift, win, tgt, v)


def weight_rows(conv_first, conv_last):
    both = jnp.concatenate(
        [conv_first.reshape(G, 216).T, conv_last.reshape(G, 27).T, jnp.zeros((5, G), BF16)], 0
    )
    return jnp.repeat(both.astype(F32), 32, axis=1)


MESH = pl.DeviceIdType.MESH
REACH = 4
ORDER = (0, 1, 4, 3, 2)


def gather_kernel(feat, pts, win, tgt, allpts, send, recv, relay_send, psend, precv, own):
    f = lax.axis_index("frame")
    r = lax.axis_index("row")
    frames = lax.axis_size("frame")
    rows = lax.axis_size("row")
    core = r % 2
    barrier = pltpu.get_barrier_semaphore()

    def greet(there_f, there_r):
        pl.semaphore_signal(
            barrier, inc=1, device_id={"frame": there_f, "row": there_r}, device_id_type=MESH
        )

    for off in range(1, rows):
        greet(f, (r + off) % rows)
    for j in range(1, REACH + 1):
        pl.when(f + j < frames)(lambda j=j: greet(f + j, r))
        pl.when(f - j >= 0)(lambda j=j: greet(f - j, r))
    later = jnp.minimum(frames - 1 - f, REACH)
    earlier = jnp.minimum(f, REACH)
    pl.semaphore_wait(barrier, rows - 1 + later + earlier)

    def frame_copy(j, there):
        return pltpu.make_async_remote_copy(
            src_ref=feat,
            dst_ref=win.at[2, j],
            send_sem=send.at[0, j],
            recv_sem=recv.at[2, j],
            device_id={"frame": there, "row": r},
            device_id_type=MESH,
        )

    def row_copy(lane, j, q, there, src=None):
        return pltpu.make_async_remote_copy(
            src_ref=(feat if j == 0 else win.at[2, j]) if src is None else src,
            dst_ref=win.at[q, j],
            send_sem=send.at[lane, j] if src is None else relay_send.at[j],
            recv_sem=recv.at[q, j],
            device_id={"frame": f, "row": there},
            device_id_type=MESH,
        )

    def point_copy(off):
        there = (r + off) % rows
        return pltpu.make_async_remote_copy(
            src_ref=pts,
            dst_ref=allpts.at[r],
            send_sem=psend.at[off],
            recv_sem=precv.at[r],
            device_id={"frame": f, "row": there},
            device_id_type=MESH,
        )

    def point_arrival(off):
        there = (r + off) % rows
        return pltpu.make_async_remote_copy(
            src_ref=pts,
            dst_ref=allpts.at[there],
            send_sem=psend.at[off],
            recv_sem=precv.at[there],
            device_id={"frame": f, "row": there},
            device_id_type=MESH,
        )

    routes = {0: ((1, 1, 1), (2, 0, 2), (3, 3, -1)), 1: ((1, 3, -1), (2, 1, 1), (3, 4, -2))}
    relays = {0: (1, 0, 1), 1: (3, 4, -1)}

    def inside(there):
        return (there >= 0) & (there < rows)

    def row_sends(j, act):
        for c in range(2):
            for lane, q, off in routes[c]:
                ok = (core == c) & inside(r + off) & (f >= j)
                pl.when(ok)(lambda lane=lane, q=q, off=off: act(row_copy(lane, j, q, r + off)))

    def relay(j, act, wait_first):
        for c in range(2):
            here, q, off = relays[c]
            source = r - 1 if c == 0 else r + 1
            ok = (core == c) & inside(source) & (f >= j)

            def body(here=here, q=q, off=off):
                if wait_first:
                    row_copy(1, j, here, r + off).wait_recv()
                act(row_copy(0, j, q, r + off, src=win.at[here, j]))

            pl.when(ok)(body)

    def start(copy):
        copy.start()

    mine = pltpu.make_async_copy(feat, win.at[2, 0], own.at[0])
    mine_pts = pltpu.make_async_copy(pts, allpts.at[r], own.at[1])
    mine.start()
    mine_pts.start()
    for j in (1, 4, 3, 2):
        pl.when(f + j < frames)(lambda j=j: frame_copy(j, f + j).start())
    row_sends(0, start)
    for off in range(1, rows):
        point_copy(off).start()
    for n, j in enumerate(ORDER):
        if j:
            pl.when(f >= j)(lambda j=j: frame_copy(j, f).wait_recv())
            row_sends(j, start)
        if n:
            relay(ORDER[n - 1], start, True)
    relay(ORDER[-1], start, True)
    for off in range(1, rows):
        point_arrival(off).wait_recv()
    mine_pts.wait()
    for s in range(2):
        tgt[s] = count_points(allpts, s, r, rows)

    for j in ORDER:
        for c, slots in ((0, ((0, -2), (3, 1), (4, 2))), (1, ((0, -2), (1, -1), (4, 2)))):
            for q, off in slots:
                ok = (core == c) & inside(r + off) & (f >= j)
                pl.when(ok)(lambda q=q, j=j: row_copy(1, j, q, r).wait_recv())
    for j in range(1, REACH + 1):
        pl.when(f + j < frames)(lambda j=j: frame_copy(j, f + j).wait_send())
    for j in ORDER:
        row_sends(j, lambda copy: copy.wait_send())
        relay(j, lambda copy: copy.wait_send(), False)
    for off in range(1, rows):
        point_copy(off).wait_send()
    mine.wait()


def gather(features, points):
    frames, rows, cols, chans = features.shape
    count = lax.axis_size("row")
    vmem = pl.BlockSpec(memory_space=pltpu.VMEM)
    hbm = pl.BlockSpec(memory_space=pl.ANY)
    dma = pltpu.SemaphoreType.DMA
    return pl.pallas_call(
        gather_kernel,
        out_shape=(
            jax.ShapeDtypeStruct((5, REACH + 1) + features.shape, features.dtype),
            jax.ShapeDtypeStruct((2, 104, 256), F32),
        ),
        in_specs=[vmem, vmem],
        out_specs=(hbm, vmem),
        scratch_shapes=[
            pltpu.VMEM((count,) + points.shape, points.dtype),
            dma((4, REACH + 1)),
            dma((5, REACH + 1)),
            dma((REACH + 1,)),
            dma((count,)),
            dma((count,)),
            dma((2,)),
        ],
        compiler_params=pltpu.CompilerParams(collective_id=0, has_side_effects=True),
        name="gather_window",
    )(features, points)


def shards(features, row_shift, lidar_points, conv_first, conv_last):
    pos = jnp.stack([lax.axis_index("frame"), lax.axis_index("row")]).astype(I32)
    win, tgt = gather(features, lidar_points.astype(BF16))
    return local_compute(pos, row_shift, win, tgt, weight_rows(conv_first, conv_last))


def solution(mesh):
    P = jax.sharding.PartitionSpec
    out = P("frame", None, "row", None)
    return jax.shard_map(
        shards,
        mesh=mesh,
        in_specs=(P("frame", "row", None, None), P(), P("frame", None, "row"), P(), P()),
        out_specs=(out, out),
        check_vma=False,
    )
```

```python
import functools
import math

import jax
import jax.numpy as jnp
from jax import lax
from jax.experimental import pallas as pl
from jax.experimental.pallas import tpu as pltpu

G = 8
D = 96
HIST = 8
W = 128
TILES = 4
STEP = D // TILES
F32, BF16, I32 = jnp.float32, jnp.bfloat16, jnp.int32
NT = (((1,), (1,)), ((), ()))
PAIRS = ((8, 2, 6), (7, 1, 6), (6, 3, 5), (5, 4, 4))
SCALE = 1.0 / math.sqrt(HIST * 16)


def iota(shape, dim):
    return lax.broadcasted_iota(I32, shape, dim)


def build_tables(first_ref, last_ref, v1, v2, t1, t2, band, pick, back):
    grow = jnp.where(iota((G, 256), 1) // 32 == iota((G, 256), 0), 1.0, 0.0).astype(BF16)
    tn = (((0,), (0,)), ((), ()))
    for a in range(3):
        for b in range(3):
            for e in range(3):
                w = first_ref[a, b, e]
                v1[(a * 3 + b) * 3 + e] = lax.dot_general(w, grow, tn, preferred_element_type=F32)
            v2[a * 3 + b] = jnp.dot(last_ref[a, b], grow, preferred_element_type=F32)
    m = iota((32, 256), 1) % 32
    li = iota((32, 256), 0)
    masks = [(li == m + a) & (m < STEP + 2) for a in range(3)]

    def first(b, c):
        for e in range(3):
            for i in range(G):
                block = jnp.zeros((32, 256), F32)
                for a in range(3):
                    row = v1[a * 9 + e + 3 * b, i : i + 1, :]
                    block = jnp.where(masks[a], row, block)
                at = (e * G + i) * 32
                t1[0, b, at : at + 32, :] = block.astype(BF16)
        return c

    lax.fori_loop(0, 3, first, 0)
    rows2 = [(m == li + a) & (li < STEP) for a in range(3)]

    def last(b, c):
        for e in range(3):
            block = jnp.zeros((32, 256), F32)
            for a in range(3):
                row = v2[a * 3 + b, e : e + 1, :]
                block = jnp.where(rows2[a], row, block)
            t2[b, e * 32 : e * 32 + 32, :] = block.astype(BF16)
        return c

    lax.fori_loop(0, 3, last, 0)

    lane = iota((W, W), 1)
    w = iota((W, W), 0)
    for p, (ka, kb, turn) in enumerate(PAIRS):
        for n, (k, base) in enumerate(((ka, 0), (kb, 16 * turn))):
            s = (lane + w + 1 - base) & (W - 1)
            ok = (s < 12 * k) & (s <= w)
            band[p, n] = jnp.where(ok, 1.0, 0.0).astype(BF16)
    for gq in range(4):
        low = lane % 32
        d = STEP * ((lane // 32 - gq + 4) % 4) - 2 + low
        real = (low < STEP + 4) & (d >= 0) & (d < D)
        for p, (ka, kb, turn) in enumerate(PAIRS):
            hit = (w == (((d * ka) >> 3) + W - 1) % W) | (w == (((d * kb) >> 3) + 16 * turn - 1) % W)
            pick[gq, p * W : (p + 1) * W, :] = jnp.where(hit & real, 1.0, 0.0).astype(BF16)
    back[...] = jnp.where(lane + w == W - 1, 1.0, 0.0).astype(BF16)

    def turned(b, c):
        for j in range(1, TILES):
            for e in range(3):
                for h in range(2):
                    for q in range(4):
                        at = e * 256 + h * W
                        t1[j, b, at + q * 32 : at + q * 32 + 32, :] = t1[
                            0, b, at + ((q - j) % 4) * 32 : at + ((q - j) % 4) * 32 + 32, :
                        ]
        return c

    lax.fori_loop(0, 3, turned, 0)


def compute_kernel(
    pos, shift, win, tgt, first_ref, last_ref, occ, grad, v1, v2, t1, t2, band, pick, back, qm, kbuf, skew, pad, x3, hid
):
    slot = pl.program_id(0)
    if pos is None:
        frame, row = lax.axis_index("frame"), lax.axis_index("row")
    else:
        frame, row = pos[0], pos[1]
    t = 2 * frame + slot

    @pl.when(slot == 0)
    def _():
        build_tables(first_ref, last_ref, v1, v2, t1, t2, band, pick, back)

    lane = iota((W, W), 1)
    for s in range(2 * TILES):
        pad[s, 0:8, :] = jnp.zeros((8, W), F32)
        pad[s, 136:144, :] = jnp.zeros((8, W), F32)

    def cost_row(ro, c):
        rr = ro + 2
        q = win[rr // 2, 0, slot, rr % 2]
        for g in range(G):
            qm[g * W : (g + 1) * W, :] = jnp.where(lane // 16 == g, q, jnp.zeros_like(q))
        for p, (ka, kb, turn) in enumerate(PAIRS):
            for n, k in enumerate((ka, kb)):
                j = (k - slot + 1) // 2
                fi = slot - k + 2 * j
                rs = rr + shift[k - 1, t]
                src = 2 * row - 4 + rs
                ok = (t - k >= 0) & (src >= 0) & (src < 32)
                key = win[rs // 2, j, fi, rs % 2]
                key = jnp.where(ok, key, jnp.zeros_like(key))
                key = jnp.dot(back[...], key, preferred_element_type=F32).astype(BF16)
                if n:
                    cut = W - 16 * turn
                    kbuf[p, W + 16 * turn : 2 * W, :] = key[0:cut]
                    kbuf[p, W : W + 16 * turn, :] = key[cut:W]
                else:
                    kbuf[p, 0:W, :] = key
        for p in range(4):
            m = lax.dot_general(qm[...], kbuf[p], NT, preferred_element_type=F32)
            for g in range(G):
                rows = m[g * W : (g + 1) * W].astype(BF16)
                both = rows[:, 0:W] * band[p, 0] + rows[:, W : 2 * W] * band[p, 1]
                skew[g * W : (g + 1) * W, p * W : (p + 1) * W] = pltpu.roll(
                    both, 0, 1, stride=1, stride_axis=0
                )
        src = 2 * row - 2 + ro
        live = (src >= 0) & (src < 32)
        for h in range(2):
            picked = [
                jnp.dot(
                    skew[(4 * h + gq) * W : (4 * h + gq + 1) * W, :],
                    pick[gq],
                    preferred_element_type=F32,
                )
                for gq in range(4)
            ]
            for j in range(TILES):
                x = picked[0]
                for gq in range(1, 4):
                    x = jnp.where(lane // 32 == (j + gq) % 4, picked[gq], x)
                s = 2 * j + h
                pad[s, 8 : 8 + W, :] = jnp.where(live, x * SCALE, 0.0)
                for e in range(3):
                    at = e * 256 + h * W
                    x3[j, ro, :, at : at + W] = pad[s, 7 + e : 7 + e + W, :].astype(BF16)
        return c

    lax.fori_loop(0, 6, cost_row, 0)

    def tile(j, c):
        total = jnp.dot(x3[j, 0:4].reshape(4 * W, 768), t1[j, 0], preferred_element_type=F32)
        for b in (1, 2):
            total += jnp.dot(x3[j, b : b + 4].reshape(4 * W, 768), t1[j, b], preferred_element_type=F32)
        d = STEP * j - 1 + iota((W, 256), 1) % 32
        inside = (d >= 0) & (d < D)
        for h in range(4):
            src = 2 * row - 1 + h
            ok = inside & ((src >= 0) & (src < 32))
            hid[h] = jnp.where(ok, jnp.maximum(total[h * W : (h + 1) * W], 0.0), 0.0).astype(BF16)
        out = jnp.zeros((96, 256), F32)
        for b in range(3):
            out += lax.dot_general(t2[b], hid[b : b + 2].reshape(256, 256), NT, preferred_element_type=F32)
        for r in range(2):
            cut = out[:, r * W : (r + 1) * W]
            wl = iota((STEP, W), 1)
            logits = (
                cut[32 : 32 + STEP]
                + jnp.where(wl == 0, 0.0, pltpu.roll(cut[0:STEP], 1, 1))
                + jnp.where(wl == W - 1, 0.0, pltpu.roll(cut[64 : 64 + STEP], W - 1, 1))
            )
            sig = jax.nn.sigmoid(logits)
            ds = pl.ds(j * STEP, STEP)
            occ[0, ds, r, :] = sig.astype(BF16)
            hits = tgt[slot, D : D + 1, r * W : (r + 1) * W]
            spots = tgt[slot, pl.ds(pl.multiple_of(j * STEP, 8), STEP), r * W : (r + 1) * W]
            grad[0, ds, r, :] = hits * sig - spots
        return c

    lax.fori_loop(0, TILES, tile, 0)


def count_points(pts, slot, row, begin, count):
    n = pts.shape[3]
    one = jnp.ones((), BF16)
    zero = jnp.zeros((), BF16)
    bins = iota((104, n), 0)
    spots = iota((256, n), 0).astype(BF16)

    def points(src, total):
        p = [pts[src, c, pl.ds(slot, 1), :] for c in range(3)]
        local = p[0].astype(F32) - (2 * row).astype(F32)
        inside = (local >= 0) & (local < 2)
        code = jnp.where(inside, local * W + p[1].astype(F32), -1.0).astype(BF16)
        dep = p[2]
        left = jnp.where((bins.astype(BF16) == dep) | (bins >= D), one, zero)
        right = jnp.where(spots == code, one, zero)
        return total + lax.dot_general(left, right, NT, preferred_element_type=F32)

    return lax.fori_loop(begin, begin + count, points, jnp.zeros((104, 256), F32))


def local_compute(pos, shift, win, tgt, first, last):
    vmem = pl.BlockSpec(memory_space=pltpu.VMEM)
    smem = pl.BlockSpec(memory_space=pltpu.SMEM)
    block = pl.BlockSpec((1, D, 2, W), lambda s: (s, 0, 0, 0))
    return pl.pallas_call(
        compute_kernel if pos is not None else functools.partial(compute_kernel, None),
        grid=(2,),
        out_shape=(
            jax.ShapeDtypeStruct((2, D, 2, W), BF16),
            jax.ShapeDtypeStruct((2, D, 2, W), F32),
        ),
        in_specs=([] if pos is None else [smem]) + [smem, vmem, vmem, vmem, vmem],
        out_specs=(block, block),
        scratch_shapes=[
            pltpu.VMEM((27, G, 256), F32),
            pltpu.VMEM((9, 3, 256), F32),
            pltpu.VMEM((TILES, 3, 768, 256), BF16),
            pltpu.VMEM((3, 96, 256), BF16),
            pltpu.VMEM((4, 2, W, W), BF16),
            pltpu.VMEM((4, 4 * W, W), BF16),
            pltpu.VMEM((W, W), BF16),
            pltpu.VMEM((G * W, W), BF16),
            pltpu.VMEM((4, 2 * W, W), BF16),
            pltpu.VMEM((G * W, 4 * W), BF16),
            pltpu.VMEM((2 * TILES, 144, W), F32),
            pltpu.VMEM((TILES, 6, W, 768), BF16),
            pltpu.VMEM((4, W, 256), BF16),
        ],
        compiler_params=pltpu.CompilerParams(vmem_limit_bytes=60000 * 1024),
        name="local_compute",
    )(*([] if pos is None else [pos]), shift, win, tgt, first, last)


MESH = pl.DeviceIdType.MESH
REACH = 4
ORDER = (0, 1, 4, 3, 2)


def gather_kernel(
    feat, pts, win, tgt, allpts, detour, send, recv, relay_send, psend, precv, own, dsend, drecv
):
    f = lax.axis_index("frame")
    r = lax.axis_index("row")
    frames = lax.axis_size("frame")
    rows = lax.axis_size("row")
    core = r % 2
    half = rows // 2
    partner = (f + frames // 2) % frames

    def inside(there):
        return (there >= 0) & (there < rows)

    def crosses(off):
        return inside(r + off) & ((r + off) // half != r // half)

    barrier = pltpu.get_barrier_semaphore()

    def greet(there_f, there_r):
        pl.semaphore_signal(
            barrier, inc=1, device_id={"frame": there_f, "row": there_r}, device_id_type=MESH
        )

    for off in range(1, rows):
        greet(f, (r + off) % rows)
    for j in range(1, REACH + 1):
        pl.when(f + j < frames)(lambda j=j: greet(f + j, r))
        pl.when(f - j >= 0)(lambda j=j: greet(f - j, r))
    later = jnp.minimum(frames - 1 - f, REACH)
    earlier = jnp.minimum(f, REACH)
    crossing = jnp.int32(0)
    for off in (-2, -1, 1, 2):
        pl.when(crosses(off))(lambda off=off: greet(partner, r + off))
        crossing += crosses(off).astype(jnp.int32)
    pl.semaphore_wait(barrier, rows - 1 + later + earlier + crossing)

    def frame_copy(j, there):
        return pltpu.make_async_remote_copy(
            src_ref=feat,
            dst_ref=win.at[2, j],
            send_sem=send.at[0, j],
            recv_sem=recv.at[2, j],
            device_id={"frame": there, "row": r},
            device_id_type=MESH,
        )

    def row_copy(lane, j, q, there, src=None):
        return pltpu.make_async_remote_copy(
            src_ref=(feat if j == 0 else win.at[2, j]) if src is None else src,
            dst_ref=win.at[q, j],
            send_sem=send.at[lane, j] if src is None else relay_send.at[j],
            recv_sem=recv.at[q, j],
            device_id={"frame": f, "row": there},
            device_id_type=MESH,
        )

    def point_copy(off):
        there = (r + off) % rows
        return pltpu.make_async_remote_copy(
            src_ref=pts,
            dst_ref=allpts.at[r],
            send_sem=psend.at[off],
            recv_sem=precv.at[r],
            device_id={"frame": f, "row": there},
            device_id_type=MESH,
        )

    def point_arrival(off):
        there = (r + off) % rows
        return pltpu.make_async_remote_copy(
            src_ref=pts,
            dst_ref=allpts.at[there],
            send_sem=psend.at[off],
            recv_sem=precv.at[there],
            device_id={"frame": f, "row": there},
            device_id_type=MESH,
        )

    routes = {0: ((1, 1, 1), (2, 0, 2), (3, 3, -1)), 1: ((1, 3, -1), (2, 1, 1), (3, 4, -2))}
    relays = {0: (1, 0, 1), 1: (3, 4, -1)}

    def detour_copy(lane, j):
        return pltpu.make_async_remote_copy(
            src_ref=feat if j == 0 else win.at[2, j],
            dst_ref=detour.at[j],
            send_sem=send.at[lane, j],
            recv_sem=drecv.at[j],
            device_id={"frame": partner, "row": r},
            device_id_type=MESH,
        )

    def onward_copy(j, q, off):
        return pltpu.make_async_remote_copy(
            src_ref=detour.at[j],
            dst_ref=win.at[q, j],
            send_sem=dsend.at[j],
            recv_sem=recv.at[q, j],
            device_id={"frame": partner, "row": r + off},
            device_id_type=MESH,
        )

    def row_sends(j, act):
        for c in range(2):
            for lane, q, off in routes[c]:
                ok = (core == c) & inside(r + off) & (f >= j)
                near = ok & jnp.logical_not(crosses(off))
                pl.when(near)(lambda lane=lane, q=q, off=off: act(row_copy(lane, j, q, r + off)))
                if lane > 1:
                    pl.when(ok & crosses(off))(lambda lane=lane: act(detour_copy(lane, j)))

    def onward(j, act, wait_first):
        for c in range(2):
            for lane, q, off in routes[c][1:]:

                def body(lane=lane, q=q, off=off):
                    if wait_first:
                        detour_copy(lane, j).wait_recv()
                    act(onward_copy(j, q, off))

                pl.when((core == c) & crosses(off) & (partner >= j))(body)

    def relay(j, act, wait_first):
        for c in range(2):
            here, q, off = relays[c]
            source = r - 1 if c == 0 else r + 1
            ok = (core == c) & inside(source) & (f >= j)

            def body(here=here, q=q, off=off):
                if wait_first:
                    row_copy(1, j, here, r + off).wait_recv()
                act(row_copy(0, j, q, r + off, src=win.at[here, j]))

            pl.when(ok)(body)

    def start(copy):
        copy.start()

    mine = pltpu.make_async_copy(feat, win.at[2, 0], own.at[0])
    mine_pts = pltpu.make_async_copy(pts, allpts.at[r], own.at[1])
    for off in range(1, rows):
        point_copy(off).start()
    mine.start()
    mine_pts.start()
    row_sends(0, start)
    for j in (1, 4, 3, 2):
        pl.when(f + j < frames)(lambda j=j: frame_copy(j, f + j).start())
    for off in range(1, rows):
        point_arrival(off).wait_recv()
    mine_pts.wait()
    tgt[...] = jnp.zeros_like(tgt)
    for n, j in enumerate(ORDER):
        if j:
            pl.when(f >= j)(lambda j=j: frame_copy(j, f).wait_recv())
            row_sends(j, start)
            onward(ORDER[n - 1], start, True)
            relay(ORDER[n - 1], start, True)
            for s in range(2):
                tgt[s] += count_points(allpts, s, r, (n - 1) * (rows // 4), rows // 4)
    onward(ORDER[-1], start, True)
    relay(ORDER[-1], start, True)

    for j in ORDER:
        for c, slots in ((0, ((0, -2), (3, 1), (4, 2))), (1, ((0, -2), (1, -1), (4, 2)))):
            for q, off in slots:
                ok = (core == c) & inside(r + off) & (f >= j)
                pl.when(ok)(lambda q=q, j=j: row_copy(1, j, q, r).wait_recv())
    for j in range(1, REACH + 1):
        pl.when(f + j < frames)(lambda j=j: frame_copy(j, f + j).wait_send())
    for j in ORDER:
        row_sends(j, lambda copy: copy.wait_send())
        onward(j, lambda copy: copy.wait_send(), False)
        relay(j, lambda copy: copy.wait_send(), False)
    for off in range(1, rows):
        point_copy(off).wait_send()
    mine.wait()


def gather(features, points):
    frames, rows, cols, chans = features.shape
    count = lax.axis_size("row")
    vmem = pl.BlockSpec(memory_space=pltpu.VMEM)
    hbm = pl.BlockSpec(memory_space=pl.ANY)
    dma = pltpu.SemaphoreType.DMA
    return pl.pallas_call(
        gather_kernel,
        out_shape=(
            jax.ShapeDtypeStruct((5, REACH + 1) + features.shape, features.dtype),
            jax.ShapeDtypeStruct((2, 104, 256), F32),
        ),
        in_specs=[vmem, vmem],
        out_specs=(hbm, vmem),
        scratch_shapes=[
            pltpu.VMEM((count,) + points.shape, points.dtype),
            pltpu.VMEM((REACH + 1,) + features.shape, features.dtype),
            dma((4, REACH + 1)),
            dma((5, REACH + 1)),
            dma((REACH + 1,)),
            dma((count,)),
            dma((count,)),
            dma((2,)),
            dma((REACH + 1,)),
            dma((REACH + 1,)),
        ],
        compiler_params=pltpu.CompilerParams(collective_id=0, has_side_effects=True),
        name="gather_window",
    )(features, points)


def shards(features, row_shift, lidar_points, conv_first, conv_last):
    points = jnp.transpose(lidar_points, (1, 0, 2)).astype(BF16)
    win, tgt = gather(features, points)
    first = jnp.transpose(conv_first, (2, 3, 4, 0, 1))
    last = jnp.transpose(conv_last[0], (1, 2, 3, 0))
    return local_compute(None, row_shift.T, win, tgt, first, last)


def solution(mesh):
    P = jax.sharding.PartitionSpec
    out = P("frame", None, "row", None)
    return jax.shard_map(
        shards,
        mesh=mesh,
        in_specs=(P("frame", "row", None, None), P(), P("frame", None, "row"), P(), P()),
        out_specs=(out, out),
        check_vma=False,
    )
```

```python
import functools
import math

import jax
import jax.numpy as jnp
from jax import lax
from jax.experimental import pallas as pl
from jax.experimental.pallas import tpu as pltpu

G = 8
D = 96
HIST = 8
W = 128
TILES = 4
STEP = D // TILES
F32, BF16, I32 = jnp.float32, jnp.bfloat16, jnp.int32
NT = (((1,), (1,)), ((), ()))
PAIRS = ((8, 2, 6), (7, 1, 6), (6, 3, 5), (5, 4, 4))
SCALE = 1.0 / math.sqrt(HIST * 16)


def iota(shape, dim):
    return lax.broadcasted_iota(I32, shape, dim)


def build_tables(first_ref, last_ref, v1, v2, t1, t2, band, pick, back):
    grow = jnp.where(iota((G, 256), 1) // 32 == iota((G, 256), 0), 1.0, 0.0).astype(BF16)
    tn = (((0,), (0,)), ((), ()))
    for a in range(3):
        for b in range(3):
            for e in range(3):
                w = first_ref[a, b, e]
                v1[(a * 3 + b) * 3 + e] = lax.dot_general(w, grow, tn, preferred_element_type=F32)
            v2[a * 3 + b] = jnp.dot(last_ref[a, b], grow, preferred_element_type=F32)
    m = iota((32, 256), 1) % 32
    li = iota((32, 256), 0)
    masks = [(li == m + a) & (m < STEP + 2) for a in range(3)]

    def first(b, c):
        for e in range(3):
            for i in range(G):
                block = jnp.zeros((32, 256), F32)
                for a in range(3):
                    row = v1[a * 9 + e + 3 * b, i : i + 1, :]
                    block = jnp.where(masks[a], row, block)
                at = (e * G + i) * 32
                t1[0, b, at : at + 32, :] = block.astype(BF16)
        return c

    lax.fori_loop(0, 3, first, 0)
    rows2 = [(m == li + a) & (li < STEP) for a in range(3)]

    def last(b, c):
        for e in range(3):
            block = jnp.zeros((32, 256), F32)
            for a in range(3):
                row = v2[a * 3 + b, e : e + 1, :]
                block = jnp.where(rows2[a], row, block)
            t2[b, e * 32 : e * 32 + 32, :] = block.astype(BF16)
        return c

    lax.fori_loop(0, 3, last, 0)

    lane = iota((W, W), 1)
    w = iota((W, W), 0)
    for p, (ka, kb, turn) in enumerate(PAIRS):
        for n, (k, base) in enumerate(((ka, 0), (kb, 16 * turn))):
            s = (lane + w + 1 - base) & (W - 1)
            ok = (s < 12 * k) & (s <= w)
            band[p, n] = jnp.where(ok, 1.0, 0.0).astype(BF16)
    for gq in range(4):
        low = lane % 32
        d = STEP * ((lane // 32 - gq + 4) % 4) - 2 + low
        real = (low < STEP + 4) & (d >= 0) & (d < D)
        for p, (ka, kb, turn) in enumerate(PAIRS):
            hit = (w == (((d * ka) >> 3) + W - 1) % W) | (w == (((d * kb) >> 3) + 16 * turn - 1) % W)
            pick[gq, p * W : (p + 1) * W, :] = jnp.where(hit & real, 1.0, 0.0).astype(BF16)
    back[...] = jnp.where(lane + w == W - 1, 1.0, 0.0).astype(BF16)

    def turned(b, c):
        for j in range(1, TILES):
            for e in range(3):
                for h in range(2):
                    for q in range(4):
                        at = e * 256 + h * W
                        t1[j, b, at + q * 32 : at + q * 32 + 32, :] = t1[
                            0, b, at + ((q - j) % 4) * 32 : at + ((q - j) % 4) * 32 + 32, :
                        ]
        return c

    lax.fori_loop(0, 3, turned, 0)


def count_points(pts, slot, row, begin, count):
    n = pts.shape[3]
    one = jnp.ones((), BF16)
    zero = jnp.zeros((), BF16)
    bins = iota((104, n), 0)
    spots = iota((256, n), 0).astype(BF16)

    def points(src, total):
        p = [pts[src, c, pl.ds(slot, 1), :] for c in range(3)]
        local = p[0].astype(F32) - (2 * row).astype(F32)
        inside = (local >= 0) & (local < 2)
        code = jnp.where(inside, local * W + p[1].astype(F32), -1.0).astype(BF16)
        dep = p[2]
        left = jnp.where((bins.astype(BF16) == dep) | (bins >= D), one, zero)
        right = jnp.where(spots == code, one, zero)
        return total + lax.dot_general(left, right, NT, preferred_element_type=F32)

    return lax.fori_loop(begin, begin + count, points, jnp.zeros((104, 256), F32))


def build_queries(win0, qm):
    lane = iota((W, W), 1)

    def one(n, c):
        slot = n // 6
        rr = n % 6 + 2
        q = win0[rr // 2, slot, rr % 2]
        for g in range(G):
            qm[n, g * W : (g + 1) * W, :] = jnp.where(lane // 16 == g, q, jnp.zeros_like(q))
        return c

    lax.fori_loop(0, 12, one, 0)


def score(slot, p, frame, row, shift, win, band, back, qm, kbuf, skew):
    t = 2 * frame + slot
    ka, kb, turn = PAIRS[p]

    def one(ro, c):
        for n, k in enumerate((ka, kb)):
            j = (k - slot + 1) // 2
            fi = slot - k + 2 * j
            rs = ro + 2 + shift[k - 1, t]
            src = 2 * row - 4 + rs
            ok = (t - k >= 0) & (src >= 0) & (src < 32)
            key = win[j][rs // 2, fi, rs % 2]
            key = jnp.where(ok, key, jnp.zeros_like(key))
            key = jnp.dot(back[...], key, preferred_element_type=F32).astype(BF16)
            if n:
                cut = W - 16 * turn
                kbuf[W + 16 * turn : 2 * W, :] = key[0:cut]
                kbuf[W : W + 16 * turn, :] = key[cut:W]
            else:
                kbuf[0:W, :] = key
        at = slot * 6 + ro
        m = lax.dot_general(qm[at], kbuf[...], NT, preferred_element_type=F32)
        for g in range(G):
            rows = m[g * W : (g + 1) * W].astype(BF16)
            both = rows[:, 0:W] * band[p, 0] + rows[:, W : 2 * W] * band[p, 1]
            skew[at, g * W : (g + 1) * W, p * W : (p + 1) * W] = pltpu.roll(
                both, 0, 1, stride=1, stride_axis=0
            )
        return c

    lax.fori_loop(0, 6, one, 0)


def finish(slot, row, tgt, occ, grad, t1, t2, pick, skew, pad, x3, hid):
    lane = iota((W, W), 1)

    def cost_row(ro, c):
        src = 2 * row - 2 + ro
        live = (src >= 0) & (src < 32)
        for h in range(2):
            picked = [
                jnp.dot(
                    skew[slot * 6 + ro, (4 * h + gq) * W : (4 * h + gq + 1) * W, :],
                    pick[gq],
                    preferred_element_type=F32,
                )
                for gq in range(4)
            ]
            for j in range(TILES):
                x = picked[0]
                for gq in range(1, 4):
                    x = jnp.where(lane // 32 == (j + gq) % 4, picked[gq], x)
                s = 2 * j + h
                pad[s, 8 : 8 + W, :] = jnp.where(live, x * SCALE, 0.0)
                for e in range(3):
                    at = e * 256 + h * W
                    x3[j, ro, :, at : at + W] = pad[s, 7 + e : 7 + e + W, :].astype(BF16)
        return c

    lax.fori_loop(0, 6, cost_row, 0)

    def tile(j, c):
        total = jnp.dot(x3[j, 0:4].reshape(4 * W, 768), t1[j, 0], preferred_element_type=F32)
        for b in (1, 2):
            total += jnp.dot(x3[j, b : b + 4].reshape(4 * W, 768), t1[j, b], preferred_element_type=F32)
        d = STEP * j - 1 + iota((W, 256), 1) % 32
        inside = (d >= 0) & (d < D)
        for h in range(4):
            src = 2 * row - 1 + h
            ok = inside & ((src >= 0) & (src < 32))
            hid[h] = jnp.where(ok, jnp.maximum(total[h * W : (h + 1) * W], 0.0), 0.0).astype(BF16)
        out = jnp.zeros((96, 256), F32)
        for b in range(3):
            out += lax.dot_general(t2[b], hid[b : b + 2].reshape(256, 256), NT, preferred_element_type=F32)
        for r in range(2):
            cut = out[:, r * W : (r + 1) * W]
            wl = iota((STEP, W), 1)
            logits = (
                cut[32 : 32 + STEP]
                + jnp.where(wl == 0, 0.0, pltpu.roll(cut[0:STEP], 1, 1))
                + jnp.where(wl == W - 1, 0.0, pltpu.roll(cut[64 : 64 + STEP], W - 1, 1))
            )
            sig = jax.nn.sigmoid(logits)
            ds = pl.ds(j * STEP, STEP)
            occ[slot, ds, r, :] = sig.astype(BF16)
            hits = tgt[slot, D : D + 1, r * W : (r + 1) * W]
            spots = tgt[slot, pl.ds(pl.multiple_of(j * STEP, 8), STEP), r * W : (r + 1) * W]
            grad[slot, ds, r, :] = hits * sig - spots
        return c

    lax.fori_loop(0, TILES, tile, 0)


MESH = pl.DeviceIdType.MESH
REACH = 4
ORDER = (0, 1, 4, 3, 2)


def fused_kernel(*refs):
    feat, pts, shift, first_ref, last_ref, occ, grad = refs[:7]
    win = refs[7 : 8 + REACH]
    allpts, v1, v2, t1, t2, band, pick, back, qm, kbuf, skew, pad, x3, hid, tgt = refs[8 + REACH : 23 + REACH]
    send, recv, relay_send, psend, precv, own = refs[23 + REACH :]
    f = lax.axis_index("frame")
    r = lax.axis_index("row")
    frames = lax.axis_size("frame")
    rows = lax.axis_size("row")
    core = r % 2
    def inside(there):
        return (there >= 0) & (there < rows)

    barrier = pltpu.get_barrier_semaphore()

    def greet(there_f, there_r):
        pl.semaphore_signal(
            barrier, inc=1, device_id={"frame": there_f, "row": there_r}, device_id_type=MESH
        )

    for off in range(1, rows):
        greet(f, (r + off) % rows)
    for j in range(1, REACH + 1):
        pl.when(f + j < frames)(lambda j=j: greet(f + j, r))
        pl.when(f - j >= 0)(lambda j=j: greet(f - j, r))
    later = jnp.minimum(frames - 1 - f, REACH)
    earlier = jnp.minimum(f, REACH)
    pl.semaphore_wait(barrier, rows - 1 + later + earlier)

    def frame_copy(j, there):
        return pltpu.make_async_remote_copy(
            src_ref=feat,
            dst_ref=win[j].at[2],
            send_sem=send.at[0, j],
            recv_sem=recv.at[2, j],
            device_id={"frame": there, "row": r},
            device_id_type=MESH,
        )

    def row_copy(lane, j, q, there, src=None):
        return pltpu.make_async_remote_copy(
            src_ref=(feat if j == 0 else win[j].at[2]) if src is None else src,
            dst_ref=win[j].at[q],
            send_sem=send.at[lane, j] if src is None else relay_send.at[j],
            recv_sem=recv.at[q, j],
            device_id={"frame": f, "row": there},
            device_id_type=MESH,
        )

    def point_copy(off):
        there = (r + off) % rows
        return pltpu.make_async_remote_copy(
            src_ref=pts,
            dst_ref=allpts.at[r],
            send_sem=psend.at[off],
            recv_sem=precv.at[r],
            device_id={"frame": f, "row": there},
            device_id_type=MESH,
        )

    def point_arrival(off):
        there = (r + off) % rows
        return pltpu.make_async_remote_copy(
            src_ref=pts,
            dst_ref=allpts.at[there],
            send_sem=psend.at[off],
            recv_sem=precv.at[there],
            device_id={"frame": f, "row": there},
            device_id_type=MESH,
        )

    routes = {0: ((1, 1, 1), (2, 0, 2), (3, 3, -1)), 1: ((1, 3, -1), (2, 1, 1), (3, 4, -2))}
    relays = {0: (1, 0, 1), 1: (3, 4, -1)}

    def row_sends(j, act):
        for c in range(2):
            for lane, q, off in routes[c]:
                ok = (core == c) & inside(r + off) & (f >= j)
                pl.when(ok)(lambda lane=lane, q=q, off=off: act(row_copy(lane, j, q, r + off)))

    def relay(j, act, wait_first):
        for c in range(2):
            here, q, off = relays[c]
            source = r - 1 if c == 0 else r + 1
            ok = (core == c) & inside(source) & (f >= j)

            def body(here=here, q=q, off=off):
                if wait_first:
                    row_copy(1, j, here, r + off).wait_recv()
                act(row_copy(0, j, q, r + off, src=win[j].at[here]))

            pl.when(ok)(body)

    def start(copy):
        copy.start()

    def arrive(j):
        for c, slots in ((0, ((0, -2), (3, 1), (4, 2))), (1, ((0, -2), (1, -1), (4, 2)))):
            for q, off in slots:
                ok = (core == c) & inside(r + off) & (f >= j)
                pl.when(ok)(lambda q=q: row_copy(1, j, q, r).wait_recv())

    def step(j):
        pl.when(f >= j)(lambda: frame_copy(j, f).wait_recv())
        row_sends(j, start)

    def count(s, part):
        tgt[s] += count_points(allpts, s, r, part * (rows // 4), rows // 4)

    def scores(slot, p):
        score(slot, p, f, r, shift, win, band, back, qm, kbuf, skew)

    mine = pltpu.make_async_copy(feat, win[0].at[2], own.at[0])
    mine_pts = pltpu.make_async_copy(pts, allpts.at[r], own.at[1])
    for off in range(1, rows):
        point_copy(off).start()
    mine.start()
    mine_pts.start()
    row_sends(0, start)
    for j in (1, 4, 3, 2):
        pl.when(f + j < frames)(lambda j=j: frame_copy(j, f + j).start())
    build_tables(first_ref, last_ref, v1, v2, t1, t2, band, pick, back)
    for s in range(2 * TILES):
        pad[s, 0:8, :] = jnp.zeros((8, W), F32)
        pad[s, 136:144, :] = jnp.zeros((8, W), F32)
    tgt[...] = jnp.zeros_like(tgt)
    step(1)
    step(4)
    relay(0, start, True)
    for off in range(1, rows):
        point_arrival(off).wait_recv()
    mine.wait()
    mine_pts.wait()
    for part in range(2):
        count(0, part)
    step(3)
    relay(1, start, True)
    for part in range(2, 4):
        count(0, part)
    step(2)
    relay(4, start, True)
    for part in range(2):
        count(1, part)
    relay(3, start, True)
    for part in range(2, 4):
        count(1, part)
    arrive(0)
    build_queries(win[0], qm)
    arrive(1)
    arrive(4)
    scores(0, 0)
    scores(0, 1)
    scores(1, 0)
    relay(2, start, True)
    arrive(3)
    scores(1, 1)
    scores(1, 2)
    arrive(2)
    scores(0, 2)
    scores(0, 3)
    scores(1, 3)

    def last(slot, c):
        finish(slot, r, tgt, occ, grad, t1, t2, pick, skew, pad, x3, hid)
        return c

    lax.fori_loop(0, 2, last, 0)

    for j in range(1, REACH + 1):
        pl.when(f + j < frames)(lambda j=j: frame_copy(j, f + j).wait_send())
    for j in ORDER:
        row_sends(j, lambda copy: copy.wait_send())
        relay(j, lambda copy: copy.wait_send(), False)
    for off in range(1, rows):
        point_copy(off).wait_send()


def shards(features, row_shift, lidar_points, conv_first, conv_last):
    points = jnp.transpose(lidar_points, (1, 0, 2)).astype(BF16)
    first = jnp.transpose(conv_first, (2, 3, 4, 0, 1))
    last = jnp.transpose(conv_last[0], (1, 2, 3, 0))
    count = lax.axis_size("row")
    vmem = pl.BlockSpec(memory_space=pltpu.VMEM)
    smem = pl.BlockSpec(memory_space=pltpu.SMEM)
    dma = pltpu.SemaphoreType.DMA
    return pl.pallas_call(
        fused_kernel,
        out_shape=(
            jax.ShapeDtypeStruct((2, D, 2, W), BF16),
            jax.ShapeDtypeStruct((2, D, 2, W), F32),
        ),
        in_specs=[vmem, vmem, smem, vmem, vmem],
        out_specs=(vmem, vmem),
        scratch_shapes=[pltpu.VMEM((5,) + features.shape, BF16) for _ in range(REACH + 1)]
        + [
            pltpu.VMEM((count,) + points.shape, BF16),
            pltpu.VMEM((27, G, 256), F32),
            pltpu.VMEM((9, 3, 256), F32),
            pltpu.VMEM((TILES, 3, 768, 256), BF16),
            pltpu.VMEM((3, 96, 256), BF16),
            pltpu.VMEM((4, 2, W, W), BF16),
            pltpu.VMEM((4, 4 * W, W), BF16),
            pltpu.VMEM((W, W), BF16),
            pltpu.VMEM((12, G * W, W), BF16),
            pltpu.VMEM((2 * W, W), BF16),
            pltpu.VMEM((12, G * W, 4 * W), BF16),
            pltpu.VMEM((2 * TILES, 144, W), F32),
            pltpu.VMEM((TILES, 6, W, 768), BF16),
            pltpu.VMEM((4, W, 256), BF16),
            pltpu.VMEM((2, 104, 256), F32),
            dma((4, REACH + 1)),
            dma((5, REACH + 1)),
            dma((REACH + 1,)),
            dma((count,)),
            dma((count,)),
            dma((2,)),
        ],
        compiler_params=pltpu.CompilerParams(
            collective_id=0, has_side_effects=True, vmem_limit_bytes=60000 * 1024
        ),
        name="fused_volume",
    )(features, points, row_shift.T, first, last)


def solution(mesh):
    P = jax.sharding.PartitionSpec
    out = P("frame", None, "row", None)
    return jax.shard_map(
        shards,
        mesh=mesh,
        in_specs=(P("frame", "row", None, None), P(), P("frame", None, "row"), P(), P()),
        out_specs=(out, out),
        check_vma=False,
    )
```

```python
import functools
import math

import jax
import jax.numpy as jnp
from jax import lax
from jax.experimental import pallas as pl
from jax.experimental.pallas import tpu as pltpu

G = 8
D = 96
HIST = 8
W = 128
TILES = 4
STEP = D // TILES
F32, BF16, I32 = jnp.float32, jnp.bfloat16, jnp.int32
NT = (((1,), (1,)), ((), ()))
PAIRS = ((8, 2, 6), (7, 1, 6), (6, 3, 5), (5, 4, 4))
SCALE = 1.0 / math.sqrt(HIST * 16)


def iota(shape, dim):
    return lax.broadcasted_iota(I32, shape, dim)


def build_tables(first_ref, last_ref, v1, v2, t1, t2, band, pick, back):
    grow = jnp.where(iota((G, 256), 1) // 32 == iota((G, 256), 0), 1.0, 0.0).astype(BF16)
    tn = (((0,), (0,)), ((), ()))
    for a in range(3):
        for b in range(3):
            for e in range(3):
                w = first_ref[a, b, e]
                v1[(a * 3 + b) * 3 + e] = lax.dot_general(w, grow, tn, preferred_element_type=F32)
            v2[a * 3 + b] = jnp.dot(last_ref[a, b], grow, preferred_element_type=F32)
    m = iota((32, 256), 1) % 32
    li = iota((32, 256), 0)
    masks = [(li == m + a) & (m < STEP + 2) for a in range(3)]

    def first(b, c):
        for e in range(3):
            for i in range(G):
                block = jnp.zeros((32, 256), F32)
                for a in range(3):
                    row = v1[a * 9 + e + 3 * b, i : i + 1, :]
                    block = jnp.where(masks[a], row, block)
                at = (e * G + i) * 32
                t1[0, b, at : at + 32, :] = block.astype(BF16)
        return c

    lax.fori_loop(0, 3, first, 0)
    rows2 = [(m == li + a) & (li < STEP) for a in range(3)]

    def last(b, c):
        for e in range(3):
            block = jnp.zeros((32, 256), F32)
            for a in range(3):
                row = v2[a * 3 + b, e : e + 1, :]
                block = jnp.where(rows2[a], row, block)
            t2[b, e * 32 : e * 32 + 32, :] = block.astype(BF16)
        return c

    lax.fori_loop(0, 3, last, 0)

    lane = iota((W, W), 1)
    w = iota((W, W), 0)
    for p, (ka, kb, turn) in enumerate(PAIRS):
        for n, (k, base) in enumerate(((ka, 0), (kb, 16 * turn))):
            s = (lane + w + 1 - base) & (W - 1)
            ok = (s < 12 * k) & (s <= w)
            band[p, n] = jnp.where(ok, 1.0, 0.0).astype(BF16)
    for gq in range(4):
        low = lane % 32
        d = STEP * ((lane // 32 - gq + 4) % 4) - 2 + low
        real = (low < STEP + 4) & (d >= 0) & (d < D)
        for p, (ka, kb, turn) in enumerate(PAIRS):
            hit = (w == (((d * ka) >> 3) + W - 1) % W) | (w == (((d * kb) >> 3) + 16 * turn - 1) % W)
            pick[gq, p * W : (p + 1) * W, :] = jnp.where(hit & real, 1.0, 0.0).astype(BF16)
    back[...] = jnp.where(lane + w == W - 1, 1.0, 0.0).astype(BF16)

    def turned(b, c):
        for j in range(1, TILES):
            for e in range(3):
                for h in range(2):
                    for q in range(4):
                        at = e * 256 + h * W
                        t1[j, b, at + q * 32 : at + q * 32 + 32, :] = t1[
                            0, b, at + ((q - j) % 4) * 32 : at + ((q - j) % 4) * 32 + 32, :
                        ]
        return c

    lax.fori_loop(0, 3, turned, 0)


def count_points(pts, slot, row, begin, count):
    n = pts.shape[3]
    one = jnp.ones((), BF16)
    zero = jnp.zeros((), BF16)
    bins = iota((104, n), 0)
    spots = iota((256, n), 0).astype(BF16)

    def points(src, total):
        p = [pts[src, c, pl.ds(slot, 1), :] for c in range(3)]
        local = p[0].astype(F32) - (2 * row).astype(F32)
        inside = (local >= 0) & (local < 2)
        code = jnp.where(inside, local * W + p[1].astype(F32), -1.0).astype(BF16)
        dep = p[2]
        left = jnp.where((bins.astype(BF16) == dep) | (bins >= D), one, zero)
        right = jnp.where(spots == code, one, zero)
        return total + lax.dot_general(left, right, NT, preferred_element_type=F32)

    return lax.fori_loop(begin, begin + count, points, jnp.zeros((104, 256), F32))


def build_queries(win0, qm):
    lane = iota((W, W), 1)

    def one(n, c):
        slot = n // 6
        rr = n % 6 + 2
        q = win0[rr // 2, slot, rr % 2]
        for g in range(G):
            qm[n, g * W : (g + 1) * W, :] = jnp.where(lane // 16 == g, q, jnp.zeros_like(q))
        return c

    lax.fori_loop(0, 12, one, 0)


def score(slot, p, frame, row, shift, win, band, back, qm, kbuf, skew):
    t = 2 * frame + slot
    ka, kb, turn = PAIRS[p]

    def one(ro, c):
        for n, k in enumerate((ka, kb)):
            j = (k - slot + 1) // 2
            fi = slot - k + 2 * j
            rs = ro + 2 + shift[k - 1, t]
            src = 2 * row - 4 + rs
            ok = (t - k >= 0) & (src >= 0) & (src < 32)
            key = win[j][rs // 2, fi, rs % 2]
            key = jnp.where(ok, key, jnp.zeros_like(key))
            key = jnp.dot(back[...], key, preferred_element_type=F32).astype(BF16)
            if n:
                cut = W - 16 * turn
                kbuf[ro, W + 16 * turn : 2 * W, :] = key[0:cut]
                kbuf[ro, W : W + 16 * turn, :] = key[cut:W]
            else:
                kbuf[ro, 0:W, :] = key
        at = slot * 6 + ro
        m = lax.dot_general(qm[at], kbuf[ro], NT, preferred_element_type=F32)
        for g in range(G):
            rows = m[g * W : (g + 1) * W].astype(BF16)
            both = rows[:, 0:W] * band[p, 0] + rows[:, W : 2 * W] * band[p, 1]
            skew[at, g * W : (g + 1) * W, p * W : (p + 1) * W] = pltpu.roll(
                both, 0, 1, stride=1, stride_axis=0
            )
        return c

    lax.fori_loop(0, 6, one, 0, unroll=True)


def finish(slot, row, tgt, occ, grad, t1, t2, pick, skew, pad, x3, hid):
    lane = iota((W, W), 1)

    def cost_row(ro, c):
        src = 2 * row - 2 + ro
        live = (src >= 0) & (src < 32)
        for h in range(2):
            picked = [
                jnp.dot(
                    skew[slot * 6 + ro, (4 * h + gq) * W : (4 * h + gq + 1) * W, :],
                    pick[gq],
                    preferred_element_type=F32,
                )
                for gq in range(4)
            ]
            for j in range(TILES):
                x = picked[0]
                for gq in range(1, 4):
                    x = jnp.where(lane // 32 == (j + gq) % 4, picked[gq], x)
                s = 2 * j + h
                pad[s, 8 : 8 + W, :] = jnp.where(live, x * SCALE, 0.0)
                for e in range(3):
                    at = e * 256 + h * W
                    x3[j, ro, :, at : at + W] = pad[s, 7 + e : 7 + e + W, :].astype(BF16)
        return c

    lax.fori_loop(0, 6, cost_row, 0, unroll=2)

    def tile(j, c):
        total = jnp.dot(x3[j, 0:4].reshape(4 * W, 768), t1[j, 0], preferred_element_type=F32)
        for b in (1, 2):
            total += jnp.dot(x3[j, b : b + 4].reshape(4 * W, 768), t1[j, b], preferred_element_type=F32)
        d = STEP * j - 1 + iota((W, 256), 1) % 32
        inside = (d >= 0) & (d < D)
        for h in range(4):
            src = 2 * row - 1 + h
            ok = inside & ((src >= 0) & (src < 32))
            hid[h] = jnp.where(ok, jnp.maximum(total[h * W : (h + 1) * W], 0.0), 0.0).astype(BF16)
        out = jnp.zeros((96, 256), F32)
        for b in range(3):
            out += lax.dot_general(t2[b], hid[b : b + 2].reshape(256, 256), NT, preferred_element_type=F32)
        for r in range(2):
            cut = out[:, r * W : (r + 1) * W]
            wl = iota((STEP, W), 1)
            logits = (
                cut[32 : 32 + STEP]
                + jnp.where(wl == 0, 0.0, pltpu.roll(cut[0:STEP], 1, 1))
                + jnp.where(wl == W - 1, 0.0, pltpu.roll(cut[64 : 64 + STEP], W - 1, 1))
            )
            sig = jax.nn.sigmoid(logits)
            ds = pl.ds(j * STEP, STEP)
            occ[slot, ds, r, :] = sig.astype(BF16)
            hits = tgt[slot, D : D + 1, r * W : (r + 1) * W]
            spots = tgt[slot, pl.ds(pl.multiple_of(j * STEP, 8), STEP), r * W : (r + 1) * W]
            grad[slot, ds, r, :] = hits * sig - spots
        return c

    lax.fori_loop(0, TILES, tile, 0)


MESH = pl.DeviceIdType.MESH
REACH = 4
ORDER = (0, 1, 4, 3, 2)
EDGE = (1, 3, 4)


def fused_kernel(*refs):
    feat, pts, shift, first_ref, last_ref, occ, grad = refs[:7]
    win = refs[7 : 8 + REACH]
    allpts, v1, v2, t1, t2, band, pick, back, qm, kbuf, skew, pad, x3, hid, tgt = refs[8 + REACH : 23 + REACH]
    send, recv, relay_send, psend, precv, own, esend = refs[23 + REACH :]
    f = lax.axis_index("frame")
    r = lax.axis_index("row")
    frames = lax.axis_size("frame")
    rows = lax.axis_size("row")
    core = r % 2
    def inside(there):
        return (there >= 0) & (there < rows)

    half = rows // 2

    def crosses(off):
        return inside(r + off) & ((r + off) // half != r // half)

    barrier = pltpu.get_barrier_semaphore()

    def greet(there_f, there_r):
        pl.semaphore_signal(
            barrier, inc=1, device_id={"frame": there_f, "row": there_r}, device_id_type=MESH
        )

    for off in range(1, rows):
        greet(f, (r + off) % rows)
    for j in range(1, REACH + 1):
        pl.when(f + j < frames)(lambda j=j: greet(f + j, r))
        pl.when(f - j >= 0)(lambda j=j: greet(f - j, r))
    later = jnp.minimum(frames - 1 - f, REACH)
    earlier = jnp.minimum(f, REACH)
    pl.semaphore_wait(barrier, rows - 1 + later + earlier)

    def frame_copy(j, there):
        return pltpu.make_async_remote_copy(
            src_ref=feat,
            dst_ref=win[j].at[2],
            send_sem=send.at[0, j],
            recv_sem=recv.at[2, j],
            device_id={"frame": there, "row": r},
            device_id_type=MESH,
        )

    def row_copy(lane, j, q, there, src=None):
        return pltpu.make_async_remote_copy(
            src_ref=(feat if j == 0 else win[j].at[2]) if src is None else src,
            dst_ref=win[j].at[q],
            send_sem=send.at[lane, j] if src is None else relay_send.at[j],
            recv_sem=recv.at[q, j],
            device_id={"frame": f, "row": there},
            device_id_type=MESH,
        )

    def point_copy(off):
        there = (r + off) % rows
        return pltpu.make_async_remote_copy(
            src_ref=pts,
            dst_ref=allpts.at[r],
            send_sem=psend.at[off],
            recv_sem=precv.at[r],
            device_id={"frame": f, "row": there},
            device_id_type=MESH,
        )

    def point_arrival(off):
        there = (r + off) % rows
        return pltpu.make_async_remote_copy(
            src_ref=pts,
            dst_ref=allpts.at[there],
            send_sem=psend.at[off],
            recv_sem=precv.at[there],
            device_id={"frame": f, "row": there},
            device_id_type=MESH,
        )

    routes = {0: ((1, 1, 1), (2, 0, 2), (3, 3, -1)), 1: ((1, 3, -1), (2, 1, 1), (3, 4, -2))}
    relays = {0: (1, 0, 1), 1: (3, 4, -1)}

    def row_sends(j, act):
        for c in range(2):
            for lane, q, off in routes[c]:
                ok = (core == c) & inside(r + off) & (f >= j)
                if j in EDGE:
                    ok = ok & jnp.logical_not(crosses(off))
                pl.when(ok)(lambda lane=lane, q=q, off=off: act(row_copy(lane, j, q, r + off)))

    def edge_sends(act):
        for edge, slots in ((half, (1, 0)), (half - 1, (3, 4))):
            for j in EDGE:
                for n, q in enumerate(slots):
                    copy = pltpu.make_async_remote_copy(
                        src_ref=win[0].at[q],
                        dst_ref=win[j].at[q],
                        send_sem=esend.at[n, j],
                        recv_sem=recv.at[q, j],
                        device_id={"frame": f + j, "row": r},
                        device_id_type=MESH,
                    )
                    pl.when((r == edge) & (f + j < frames))(lambda copy=copy: act(copy))

    def relay(j, act, wait_first):
        for c in range(2):
            here, q, off = relays[c]
            source = r - 1 if c == 0 else r + 1
            ok = (core == c) & inside(source) & (f >= j)

            def body(here=here, q=q, off=off):
                if wait_first:
                    row_copy(1, j, here, r + off).wait_recv()
                act(row_copy(0, j, q, r + off, src=win[j].at[here]))

            pl.when(ok)(body)

    def start(copy):
        copy.start()

    def arrive(j):
        for c, slots in ((0, ((0, -2), (3, 1), (4, 2))), (1, ((0, -2), (1, -1), (4, 2)))):
            for q, off in slots:
                ok = (core == c) & inside(r + off) & (f >= j)
                pl.when(ok)(lambda q=q: row_copy(1, j, q, r).wait_recv())

    def step(j):
        pl.when(f >= j)(lambda: frame_copy(j, f).wait_recv())
        row_sends(j, start)

    def count(s, part):
        tgt[s] += count_points(allpts, s, r, part * (rows // 4), rows // 4)

    def scores(slot, p):
        score(slot, p, f, r, shift, win, band, back, qm, kbuf, skew)

    mine = pltpu.make_async_copy(feat, win[0].at[2], own.at[0])
    mine_pts = pltpu.make_async_copy(pts, allpts.at[r], own.at[1])
    for off in range(1, rows):
        point_copy(off).start()
    mine.start()
    mine_pts.start()
    row_sends(0, start)
    for j in (1, 4, 3, 2):
        pl.when(f + j < frames)(lambda j=j: frame_copy(j, f + j).start())
    build_tables(first_ref, last_ref, v1, v2, t1, t2, band, pick, back)
    for s in range(2 * TILES):
        pad[s, 0:8, :] = jnp.zeros((8, W), F32)
        pad[s, 136:144, :] = jnp.zeros((8, W), F32)
    tgt[...] = jnp.zeros_like(tgt)
    step(1)
    step(4)
    relay(0, start, True)
    arrive(0)
    edge_sends(start)
    for off in range(1, rows):
        point_arrival(off).wait_recv()
    mine.wait()
    mine_pts.wait()
    for part in range(2):
        count(0, part)
    step(3)
    relay(1, start, True)
    for part in range(2, 4):
        count(0, part)
    step(2)
    relay(4, start, True)
    for part in range(2):
        count(1, part)
    relay(3, start, True)
    for part in range(2, 4):
        count(1, part)
    build_queries(win[0], qm)
    arrive(1)
    arrive(4)
    scores(0, 0)
    scores(0, 1)
    scores(1, 0)
    relay(2, start, True)
    arrive(3)
    scores(1, 1)
    scores(1, 2)
    arrive(2)
    scores(0, 2)
    scores(0, 3)
    scores(1, 3)

    def last(slot, c):
        finish(slot, r, tgt, occ, grad, t1, t2, pick, skew, pad, x3, hid)
        return c

    lax.fori_loop(0, 2, last, 0)

    for j in range(1, REACH + 1):
        pl.when(f + j < frames)(lambda j=j: frame_copy(j, f + j).wait_send())
    edge_sends(lambda copy: copy.wait_send())
    for j in ORDER:
        row_sends(j, lambda copy: copy.wait_send())
        relay(j, lambda copy: copy.wait_send(), False)
    for off in range(1, rows):
        point_copy(off).wait_send()


def shards(features, row_shift, lidar_points, conv_first, conv_last):
    points = jnp.transpose(lidar_points, (1, 0, 2)).astype(BF16)
    first = jnp.transpose(conv_first, (2, 3, 4, 0, 1))
    last = jnp.transpose(conv_last[0], (1, 2, 3, 0))
    count = lax.axis_size("row")
    vmem = pl.BlockSpec(memory_space=pltpu.VMEM)
    smem = pl.BlockSpec(memory_space=pltpu.SMEM)
    dma = pltpu.SemaphoreType.DMA
    return pl.pallas_call(
        fused_kernel,
        out_shape=(
            jax.ShapeDtypeStruct((2, D, 2, W), BF16),
            jax.ShapeDtypeStruct((2, D, 2, W), F32),
        ),
        in_specs=[vmem, vmem, smem, vmem, vmem],
        out_specs=(vmem, vmem),
        scratch_shapes=[pltpu.VMEM((5,) + features.shape, BF16) for _ in range(REACH + 1)]
        + [
            pltpu.VMEM((count,) + points.shape, BF16),
            pltpu.VMEM((27, G, 256), F32),
            pltpu.VMEM((9, 3, 256), F32),
            pltpu.VMEM((TILES, 3, 768, 256), BF16),
            pltpu.VMEM((3, 96, 256), BF16),
            pltpu.VMEM((4, 2, W, W), BF16),
            pltpu.VMEM((4, 4 * W, W), BF16),
            pltpu.VMEM((W, W), BF16),
            pltpu.VMEM((12, G * W, W), BF16),
            pltpu.VMEM((6, 2 * W, W), BF16),
            pltpu.VMEM((12, G * W, 4 * W), BF16),
            pltpu.VMEM((2 * TILES, 144, W), F32),
            pltpu.VMEM((TILES, 6, W, 768), BF16),
            pltpu.VMEM((4, W, 256), BF16),
            pltpu.VMEM((2, 104, 256), F32),
            dma((4, REACH + 1)),
            dma((5, REACH + 1)),
            dma((REACH + 1,)),
            dma((count,)),
            dma((count,)),
            dma((2,)),
            dma((2, REACH + 1)),
        ],
        compiler_params=pltpu.CompilerParams(
            collective_id=0, has_side_effects=True, vmem_limit_bytes=60000 * 1024
        ),
        name="fused_volume",
    )(features, points, row_shift.T, first, last)


def solution(mesh):
    P = jax.sharding.PartitionSpec
    out = P("frame", None, "row", None)
    return jax.shard_map(
        shards,
        mesh=mesh,
        in_specs=(P("frame", "row", None, None), P(), P("frame", None, "row"), P(), P()),
        out_specs=(out, out),
        check_vma=False,
    )
```

```python
import functools
import math

import jax
import jax.numpy as jnp
from jax import lax
from jax.experimental import pallas as pl
from jax.experimental.pallas import tpu as pltpu

G = 8
D = 96
HIST = 8
W = 128
TILES = 4
STEP = D // TILES
NROWS = 8
F32, BF16, I32 = jnp.float32, jnp.bfloat16, jnp.int32
NT = (((1,), (1,)), ((), ()))
PAIRS = ((8, 2, 6), (7, 1, 6), (6, 3, 5), (5, 4, 4))
SCALE = 1.0 / math.sqrt(HIST * 16)


def iota(shape, dim):
    return lax.broadcasted_iota(I32, shape, dim)


def build_tables(first_ref, last_ref, v1, v2, t1, t2, band, pick, back):
    grow = jnp.where(iota((G, 256), 1) // 32 == iota((G, 256), 0), 1.0, 0.0).astype(BF16)
    tn = (((0,), (0,)), ((), ()))
    for a in range(3):
        for b in range(3):
            for e in range(3):
                w = first_ref[a, b, e]
                v1[(a * 3 + b) * 3 + e] = lax.dot_general(w, grow, tn, preferred_element_type=F32)
            v2[a * 3 + b] = jnp.dot(last_ref[a, b], grow, preferred_element_type=F32)
    m = iota((32, 256), 1) % 32
    li = iota((32, 256), 0)
    masks = [(li == m + a) & (m < STEP + 2) for a in range(3)]

    def first(b, c):
        for e in range(3):
            for i in range(G):
                block = jnp.zeros((32, 256), F32)
                for a in range(3):
                    row = v1[a * 9 + e + 3 * b, i : i + 1, :]
                    block = jnp.where(masks[a], row, block)
                at = (e * G + i) * 32
                t1[0, b, at : at + 32, :] = block.astype(BF16)
        return c

    lax.fori_loop(0, 3, first, 0)
    rows2 = [(m == li + a) & (li < STEP) for a in range(3)]

    def last(b, c):
        for e in range(3):
            block = jnp.zeros((32, 256), F32)
            for a in range(3):
                row = v2[a * 3 + b, e : e + 1, :]
                block = jnp.where(rows2[a], row, block)
            t2[b, e * 32 : e * 32 + 32, :] = block.astype(BF16)
        return c

    lax.fori_loop(0, 3, last, 0)

    lane = iota((W, W), 1)
    w = iota((W, W), 0)
    for p, (ka, kb, turn) in enumerate(PAIRS):
        for n, (k, base) in enumerate(((ka, 0), (kb, 16 * turn))):
            s = (lane + w + 1 - base) & (W - 1)
            ok = (s < 12 * k) & (s <= w)
            band[p, n] = jnp.where(ok, 1.0, 0.0).astype(BF16)
    for gq in range(4):
        low = lane % 32
        d = STEP * ((lane // 32 - gq + 4) % 4) - 2 + low
        real = (low < STEP + 4) & (d >= 0) & (d < D)
        for p, (ka, kb, turn) in enumerate(PAIRS):
            hit = (w == (((d * ka) >> 3) + W - 1) % W) | (w == (((d * kb) >> 3) + 16 * turn - 1) % W)
            pick[gq, p * W : (p + 1) * W, :] = jnp.where(hit & real, 1.0, 0.0).astype(BF16)
    back[...] = jnp.where(lane + w == W - 1, 1.0, 0.0).astype(BF16)

    def turned(b, c):
        for j in range(1, TILES):
            for e in range(3):
                for h in range(2):
                    for q in range(4):
                        at = e * 256 + h * W
                        t1[j, b, at + q * 32 : at + q * 32 + 32, :] = t1[
                            0, b, at + ((q - j) % 4) * 32 : at + ((q - j) % 4) * 32 + 32, :
                        ]
        return c

    lax.fori_loop(0, 3, turned, 0)


def count_points(pts, slot, row, begin, count):
    n = pts.shape[3]
    one = jnp.ones((), BF16)
    zero = jnp.zeros((), BF16)
    bins = iota((104, n), 0)
    spots = iota((256, n), 0).astype(BF16)

    def points(src, totals):
        both = [pts[src, c].astype(F32) for c in range(3)]
        p = [jnp.where(slot == 0, x[0:1], x[1:2]) for x in both]
        left = jnp.where((bins.astype(BF16) == p[2].astype(BF16)) | (bins >= D), one, zero)
        added = []
        for half in range(2):
            local = p[0] - (4 * (row // 2) + 2 * half).astype(F32)
            inside = (local >= 0) & (local < 2)
            code = jnp.where(inside, local * W + p[1], -1.0).astype(BF16)
            right = jnp.where(spots == code, one, zero)
            added.append(
                totals[half] + lax.dot_general(left, right, NT, preferred_element_type=F32)
            )
        return tuple(added)

    nothing = jnp.zeros((104, 256), F32)
    return lax.fori_loop(begin, begin + count, points, (nothing, nothing))


def build_queries(core, win0, qm):
    lane = iota((W, W), 1)

    def one(ro, c):
        rr = ro + 2
        q = win0[rr // 2, core, rr % 2]
        for g in range(G):
            qm[ro, g * W : (g + 1) * W, :] = jnp.where(lane // 16 == g, q, jnp.zeros_like(q))
        return c

    lax.fori_loop(0, NROWS, one, 0)


def score(slot, p, frame, row, shift, win, band, back, qm, kbuf, skew):
    t = 2 * frame + slot
    ka, kb, turn = PAIRS[p]

    def one(ro, c):
        for n, k in enumerate((ka, kb)):
            j = (k - slot + 1) // 2
            fi = slot - k + 2 * j
            rs = ro + 2 + shift[k - 1, t]
            src = 4 * (row // 2) - 4 + rs
            ok = (t - k >= 0) & (src >= 0) & (src < 32)
            key = win[j][rs // 2, fi, rs % 2]
            key = jnp.where(ok, key, jnp.zeros_like(key))
            key = jnp.dot(back[...], key, preferred_element_type=F32).astype(BF16)
            if n:
                cut = W - 16 * turn
                kbuf[ro, W + 16 * turn : 2 * W, :] = key[0:cut]
                kbuf[ro, W : W + 16 * turn, :] = key[cut:W]
            else:
                kbuf[ro, 0:W, :] = key
        m = lax.dot_general(qm[ro], kbuf[ro], NT, preferred_element_type=F32)
        for g in range(G):
            rows = m[g * W : (g + 1) * W].astype(BF16)
            both = rows[:, 0:W] * band[p, 0] + rows[:, W : 2 * W] * band[p, 1]
            skew[ro, g * W : (g + 1) * W, p * W : (p + 1) * W] = pltpu.roll(
                both, 0, 1, stride=1, stride_axis=0
            )
        return c

    lax.fori_loop(0, NROWS, one, 0, unroll=True)


def finish(row, tgt, occ, grad, t1, t2, pick, skew, pad, x3, hid):
    lane = iota((W, W), 1)
    top = 4 * (row // 2)

    def cost_row(ro, c):
        src = top - 2 + ro
        live = (src >= 0) & (src < 32)
        for h in range(2):
            picked = [
                jnp.dot(
                    skew[ro, (4 * h + gq) * W : (4 * h + gq + 1) * W, :],
                    pick[gq],
                    preferred_element_type=F32,
                )
                for gq in range(4)
            ]
            for j in range(TILES):
                x = picked[0]
                for gq in range(1, 4):
                    x = jnp.where(lane // 32 == (j + gq) % 4, picked[gq], x)
                s = 2 * j + h
                pad[s, 8 : 8 + W, :] = jnp.where(live, x * SCALE, 0.0)
                for e in range(3):
                    at = e * 256 + h * W
                    x3[j, ro, :, at : at + W] = pad[s, 7 + e : 7 + e + W, :].astype(BF16)
        return c

    lax.fori_loop(0, NROWS, cost_row, 0, unroll=2)

    def tile(j, c):
        total = jnp.dot(x3[j, 0:6].reshape(6 * W, 768), t1[j, 0], preferred_element_type=F32)
        for b in (1, 2):
            total += jnp.dot(x3[j, b : b + 6].reshape(6 * W, 768), t1[j, b], preferred_element_type=F32)
        d = STEP * j - 1 + iota((W, 256), 1) % 32
        inside = (d >= 0) & (d < D)
        for h in range(6):
            src = top - 1 + h
            ok = inside & ((src >= 0) & (src < 32))
            hid[h] = jnp.where(ok, jnp.maximum(total[h * W : (h + 1) * W], 0.0), 0.0).astype(BF16)
        out = jnp.zeros((96, 512), F32)
        for b in range(3):
            out += lax.dot_general(t2[b], hid[b : b + 4].reshape(512, 256), NT, preferred_element_type=F32)
        for r in range(4):
            cut = out[:, r * W : (r + 1) * W]
            wl = iota((STEP, W), 1)
            logits = (
                cut[32 : 32 + STEP]
                + jnp.where(wl == 0, 0.0, pltpu.roll(cut[0:STEP], 1, 1))
                + jnp.where(wl == W - 1, 0.0, pltpu.roll(cut[64 : 64 + STEP], W - 1, 1))
            )
            sig = jax.nn.sigmoid(logits)
            ds = pl.ds(j * STEP, STEP)
            occ[r // 2, ds, r % 2, :] = sig.astype(BF16)
            hits = tgt[D : D + 1, r * W : (r + 1) * W]
            spots = tgt[pl.ds(pl.multiple_of(j * STEP, 8), STEP), r * W : (r + 1) * W]
            grad[r // 2, ds, r % 2, :] = hits * sig - spots
        return c

    lax.fori_loop(0, TILES, tile, 0)


MESH = pl.DeviceIdType.MESH
REACH = 4
ORDER = (0, 1, 4, 3, 2)
EDGE = (1, 3, 4)


def fused_kernel(*refs):
    feat, pts, shift, first_ref, last_ref, occ, grad = refs[:7]
    win = refs[7 : 8 + REACH]
    rest = refs[8 + REACH :]
    allpts, v1, v2, t1, t2, band, pick, back, qm, kbuf, skew, pad, x3, hid, tgt = rest[:15]
    occ_out, grad_out, send, recv, relay_send, psend, precv, own, esend, osend, orecv = rest[15:]
    f = lax.axis_index("frame")
    r = lax.axis_index("row")
    frames = lax.axis_size("frame")
    rows = lax.axis_size("row")
    core = r % 2
    sibling = r + 1 - 2 * core
    center = 2 + core

    def inside(there):
        return (there >= 0) & (there < rows)

    def crosses(off):
        return inside(r + off) & ((r + off) // (rows // 2) != r // (rows // 2))

    def by_frames(j, there):
        if j not in EDGE:
            return False
        if j == 4:
            return True
        return (there - j) // (frames // 2) == there // (frames // 2)

    barrier = pltpu.get_barrier_semaphore()

    def greet(there_f, there_r):
        pl.semaphore_signal(
            barrier, inc=1, device_id={"frame": there_f, "row": there_r}, device_id_type=MESH
        )

    for off in range(1, rows):
        greet(f, (r + off) % rows)
    for j in range(1, REACH + 1):
        pl.when(f + j < frames)(lambda j=j: greet(f + j, r))
        pl.when(f - j >= 0)(lambda j=j: greet(f - j, r))
    later = jnp.minimum(frames - 1 - f, REACH)
    earlier = jnp.minimum(f, REACH)
    pl.semaphore_wait(barrier, rows - 1 + later + earlier)

    def frame_copy(j, there):
        return pltpu.make_async_remote_copy(
            src_ref=feat,
            dst_ref=win[j].at[center],
            send_sem=send.at[0, j],
            recv_sem=recv.at[center, j],
            device_id={"frame": there, "row": r},
            device_id_type=MESH,
        )

    def row_copy(lane, j, q, there):
        return pltpu.make_async_remote_copy(
            src_ref=feat if j == 0 else win[j].at[center],
            dst_ref=win[j].at[q],
            send_sem=send.at[lane, j],
            recv_sem=recv.at[q, j],
            device_id={"frame": f, "row": there},
            device_id_type=MESH,
        )

    def relay_copy(n, j, q):
        return pltpu.make_async_remote_copy(
            src_ref=win[j].at[q],
            dst_ref=win[j].at[q],
            send_sem=relay_send.at[n, j],
            recv_sem=recv.at[q, j],
            device_id={"frame": f, "row": sibling},
            device_id_type=MESH,
        )

    def point_copy(off):
        there = (r + off) % rows
        return pltpu.make_async_remote_copy(
            src_ref=pts,
            dst_ref=allpts.at[r],
            send_sem=psend.at[off],
            recv_sem=precv.at[r],
            device_id={"frame": f, "row": there},
            device_id_type=MESH,
        )

    def point_arrival(off):
        there = (r + off) % rows
        return pltpu.make_async_remote_copy(
            src_ref=pts,
            dst_ref=allpts.at[there],
            send_sem=psend.at[off],
            recv_sem=precv.at[there],
            device_id={"frame": f, "row": there},
            device_id_type=MESH,
        )

    def row_sends(j, act):
        for lane, q, off in ((2, core, 2), (3, 4 + core, -2)):
            ok = inside(r + off) & (f >= j)
            if j in EDGE:
                ok = ok & jnp.logical_not(crosses(off) & by_frames(j, f))
            pl.when(ok)(lambda lane=lane, q=q, off=off: act(row_copy(lane, j, q, r + off)))
        pl.when(f >= j)(lambda: act(row_copy(1, j, center, sibling)))

    def edge_sends(act):
        for n, (q, off) in enumerate(((core, -2), (4 + core, 2))):
            for j in EDGE:
                copy = pltpu.make_async_remote_copy(
                    src_ref=win[0].at[q],
                    dst_ref=win[j].at[q],
                    send_sem=esend.at[n, j],
                    recv_sem=recv.at[q, j],
                    device_id={"frame": f + j, "row": r},
                    device_id_type=MESH,
                )
                ok = crosses(off) & (f + j < frames) & by_frames(j, f + j)
                pl.when(ok)(lambda copy=copy: act(copy))

    def relay(j, act, wait_first):
        for n, (q, off) in enumerate(((core, -2), (4 + core, 2))):

            def body(n=n, q=q):
                copy = relay_copy(n, j, q)
                if wait_first:
                    copy.wait_recv()
                act(copy)

            pl.when(inside(r + off) & (f >= j))(body)

    def start(copy):
        copy.start()

    def arrive(j):
        pl.when(f >= j)(lambda: row_copy(1, j, 5 - center, sibling).wait_recv())
        for q, off in ((1 - core, -2), (5 - core, 2)):
            ok = inside(r + off) & (f >= j)
            pl.when(ok)(lambda q=q: row_copy(1, j, q, sibling).wait_recv())

    def step(j):
        pl.when(f >= j)(lambda: frame_copy(j, f).wait_recv())
        row_sends(j, start)

    def count(part):
        counts = count_points(allpts, core, r, part * (rows // 4), rows // 4)
        for half in range(2):
            tgt[:, half * 256 : half * 256 + 256] += counts[half]

    def scores(slot, p):
        score(slot, p, f, r, shift, win, band, back, qm, kbuf, skew)

    mine = pltpu.make_async_copy(feat, win[0].at[center], own.at[0])
    mine_pts = pltpu.make_async_copy(pts, allpts.at[r], own.at[1])
    for off in range(1, rows):
        point_copy(off).start()
    mine.start()
    mine_pts.start()
    row_sends(0, start)
    for j in (1, 4, 3, 2):
        pl.when(f + j < frames)(lambda j=j: frame_copy(j, f + j).start())
    build_tables(first_ref, last_ref, v1, v2, t1, t2, band, pick, back)
    for s in range(2 * TILES):
        pad[s, 0:8, :] = jnp.zeros((8, W), F32)
        pad[s, 136:144, :] = jnp.zeros((8, W), F32)
    tgt[...] = jnp.zeros_like(tgt)
    step(1)
    step(4)
    relay(0, start, True)
    arrive(0)
    edge_sends(start)
    for off in range(1, rows):
        point_arrival(off).wait_recv()
    mine.wait()
    mine_pts.wait()
    count(0)
    step(3)
    relay(1, start, True)
    count(1)
    step(2)
    relay(4, start, True)
    build_queries(core, win[0], qm)
    count(2)
    relay(3, start, True)
    count(3)
    arrive(1)
    arrive(4)

    @pl.when(core == 0)
    def _():
        scores(0, 0)
        scores(0, 1)

    @pl.when(core == 1)
    def _():
        scores(1, 0)

    relay(2, start, True)
    arrive(3)

    @pl.when(core == 1)
    def _():
        scores(1, 1)
        scores(1, 2)

    arrive(2)

    @pl.when(core == 0)
    def _():
        scores(0, 2)
        scores(0, 3)

    @pl.when(core == 1)
    def _():
        scores(1, 3)

    finish(r, tgt, occ_out, grad_out, t1, t2, pick, skew, pad, x3, hid)

    def swap(n, src, dst):
        return pltpu.make_async_remote_copy(
            src_ref=src.at[1 - core],
            dst_ref=dst.at[core],
            send_sem=osend.at[n],
            recv_sem=orecv.at[n],
            device_id={"frame": f, "row": sibling},
            device_id_type=MESH,
        )

    swaps = (swap(0, occ_out, occ), swap(1, grad_out, grad))
    keeps = (
        pltpu.make_async_copy(occ_out.at[core], occ.at[core], own.at[2]),
        pltpu.make_async_copy(grad_out.at[core], grad.at[core], own.at[3]),
    )
    for copy in swaps + keeps:
        copy.start()
    for j in range(1, REACH + 1):
        pl.when(f + j < frames)(lambda j=j: frame_copy(j, f + j).wait_send())
    edge_sends(lambda copy: copy.wait_send())
    for j in ORDER:
        row_sends(j, lambda copy: copy.wait_send())
        relay(j, lambda copy: copy.wait_send(), False)
    for off in range(1, rows):
        point_copy(off).wait_send()
    for copy in swaps + keeps:
        copy.wait()


def shards(features, row_shift, lidar_points, conv_first, conv_last):
    points = jnp.transpose(lidar_points, (1, 0, 2)).astype(BF16)
    first = jnp.transpose(conv_first, (2, 3, 4, 0, 1))
    last = jnp.transpose(conv_last[0], (1, 2, 3, 0))
    count = lax.axis_size("row")
    vmem = pl.BlockSpec(memory_space=pltpu.VMEM)
    smem = pl.BlockSpec(memory_space=pltpu.SMEM)
    hbm = pl.BlockSpec(memory_space=pl.ANY)
    dma = pltpu.SemaphoreType.DMA
    return pl.pallas_call(
        fused_kernel,
        out_shape=(
            jax.ShapeDtypeStruct((2, D, 2, W), BF16),
            jax.ShapeDtypeStruct((2, D, 2, W), F32),
        ),
        in_specs=[vmem, vmem, smem, vmem, vmem],
        out_specs=(hbm, hbm),
        scratch_shapes=[pltpu.VMEM((6,) + features.shape, BF16) for _ in range(REACH + 1)]
        + [
            pltpu.VMEM((count,) + points.shape, BF16),
            pltpu.VMEM((27, G, 256), F32),
            pltpu.VMEM((9, 3, 256), F32),
            pltpu.VMEM((TILES, 3, 768, 256), BF16),
            pltpu.VMEM((3, 96, 256), BF16),
            pltpu.VMEM((4, 2, W, W), BF16),
            pltpu.VMEM((4, 4 * W, W), BF16),
            pltpu.VMEM((W, W), BF16),
            pltpu.VMEM((NROWS, G * W, W), BF16),
            pltpu.VMEM((NROWS, 2 * W, W), BF16),
            pltpu.VMEM((NROWS, G * W, 4 * W), BF16),
            pltpu.VMEM((2 * TILES, 144, W), F32),
            pltpu.VMEM((TILES, NROWS, W, 768), BF16),
            pltpu.VMEM((6, W, 256), BF16),
            pltpu.VMEM((104, 512), F32),
            pltpu.VMEM((2, D, 2, W), BF16),
            pltpu.VMEM((2, D, 2, W), F32),
            dma((4, REACH + 1)),
            dma((6, REACH + 1)),
            dma((2, REACH + 1)),
            dma((count,)),
            dma((count,)),
            dma((4,)),
            dma((2, REACH + 1)),
            dma((2,)),
            dma((2,)),
        ],
        compiler_params=pltpu.CompilerParams(
            collective_id=0, has_side_effects=True, vmem_limit_bytes=60000 * 1024
        ),
        name="fused_volume",
    )(features, points, row_shift.T, first, last)


def solution(mesh):
    P = jax.sharding.PartitionSpec
    out = P("frame", None, "row", None)
    return jax.shard_map(
        shards,
        mesh=mesh,
        in_specs=(P("frame", "row", None, None), P(), P("frame", None, "row"), P(), P()),
        out_specs=(out, out),
        check_vma=False,
    )
```

```python
import functools
import math

import jax
import jax.numpy as jnp
from jax import lax
from jax.experimental import pallas as pl
from jax.experimental.pallas import tpu as pltpu

G = 8
D = 96
HIST = 8
W = 128
TILES = 4
STEP = D // TILES
NROWS = 8
F32, BF16, I32 = jnp.float32, jnp.bfloat16, jnp.int32
NT = (((1,), (1,)), ((), ()))
PAIRS = ((8, 2, 6), (7, 1, 6), (6, 3, 5), (5, 4, 4))
SCALE = 1.0 / math.sqrt(HIST * 16)


def iota(shape, dim):
    return lax.broadcasted_iota(I32, shape, dim)


def build_tables(first_ref, last_ref, v1, v2, t1, t2, band, pick, back):
    grow = jnp.where(iota((G, 256), 1) // 32 == iota((G, 256), 0), 1.0, 0.0).astype(BF16)
    tn = (((0,), (0,)), ((), ()))
    for a in range(3):
        for b in range(3):
            for e in range(3):
                w = first_ref[a, b, e]
                v1[(a * 3 + b) * 3 + e] = lax.dot_general(w, grow, tn, preferred_element_type=F32)
            v2[a * 3 + b] = jnp.dot(last_ref[a, b], grow, preferred_element_type=F32)
    m = iota((32, 256), 1) % 32
    li = iota((32, 256), 0)
    masks = [(li == m + a) & (m < STEP + 2) for a in range(3)]

    def first(b, c):
        for e in range(3):
            for i in range(G):
                block = jnp.zeros((32, 256), F32)
                for a in range(3):
                    row = v1[a * 9 + e + 3 * b, i : i + 1, :]
                    block = jnp.where(masks[a], row, block)
                at = (e * G + i) * 32
                t1[0, b, at : at + 32, :] = block.astype(BF16)
        return c

    lax.fori_loop(0, 3, first, 0)
    rows2 = [(m == li + a) & (li < STEP) for a in range(3)]

    def last(b, c):
        for e in range(3):
            block = jnp.zeros((32, 256), F32)
            for a in range(3):
                row = v2[a * 3 + b, e : e + 1, :]
                block = jnp.where(rows2[a], row, block)
            t2[b, e * 32 : e * 32 + 32, :] = block.astype(BF16)
        return c

    lax.fori_loop(0, 3, last, 0)

    lane = iota((W, W), 1)
    w = iota((W, W), 0)
    for p, (ka, kb, turn) in enumerate(PAIRS):
        for n, (k, base) in enumerate(((ka, 0), (kb, 16 * turn))):
            s = (lane + w + 1 - base) & (W - 1)
            ok = (s < 12 * k) & (s <= w)
            band[p, n] = jnp.where(ok, 1.0, 0.0).astype(BF16)
    for gq in range(4):
        low = lane % 32
        d = STEP * ((lane // 32 - gq + 4) % 4) - 2 + low
        real = (low < STEP + 4) & (d >= 0) & (d < D)
        for p, (ka, kb, turn) in enumerate(PAIRS):
            hit = (w == (((d * ka) >> 3) + W - 1) % W) | (w == (((d * kb) >> 3) + 16 * turn - 1) % W)
            pick[gq, p * W : (p + 1) * W, :] = jnp.where(hit & real, 1.0, 0.0).astype(BF16)
    back[...] = jnp.where(lane + w == W - 1, 1.0, 0.0).astype(BF16)

    def turned(b, c):
        for j in range(1, TILES):
            for e in range(3):
                for h in range(2):
                    for q in range(4):
                        at = e * 256 + h * W
                        t1[j, b, at + q * 32 : at + q * 32 + 32, :] = t1[
                            0, b, at + ((q - j) % 4) * 32 : at + ((q - j) % 4) * 32 + 32, :
                        ]
        return c

    lax.fori_loop(0, 3, turned, 0)


def count_points(pts, slot, row, begin, count):
    n = pts.shape[3]
    one = jnp.ones((), BF16)
    zero = jnp.zeros((), BF16)
    bins = iota((104, n), 0)
    spots = iota((256, n), 0).astype(BF16)

    def points(src, totals):
        both = [pts[src, c].astype(F32) for c in range(3)]
        p = [jnp.where(slot == 0, x[0:1], x[1:2]) for x in both]
        left = jnp.where((bins.astype(BF16) == p[2].astype(BF16)) | (bins >= D), one, zero)
        added = []
        for half in range(2):
            local = p[0] - (4 * (row // 2) + 2 * half).astype(F32)
            inside = (local >= 0) & (local < 2)
            code = jnp.where(inside, local * W + p[1], -1.0).astype(BF16)
            right = jnp.where(spots == code, one, zero)
            added.append(
                totals[half] + lax.dot_general(left, right, NT, preferred_element_type=F32)
            )
        return tuple(added)

    nothing = jnp.zeros((104, 256), F32)
    return lax.fori_loop(begin, begin + count, points, (nothing, nothing), unroll=2)


def build_queries(core, win0, qm):
    lane = iota((W, W), 1)

    def one(ro, c):
        rr = ro + 2
        q = win0[rr // 2, core, rr % 2]
        for g in range(G):
            qm[ro, g * W : (g + 1) * W, :] = jnp.where(lane // 16 == g, q, jnp.zeros_like(q))
        return c

    lax.fori_loop(0, NROWS, one, 0)


def score(slot, p, frame, row, shift, win, band, back, qm, kbuf, skew):
    t = 2 * frame + slot
    ka, kb, turn = PAIRS[p]

    def one(ro, c):
        for n, k in enumerate((ka, kb)):
            j = (k - slot + 1) // 2
            fi = slot - k + 2 * j
            rs = ro + 2 + shift[k - 1, t]
            src = 4 * (row // 2) - 4 + rs
            ok = (t - k >= 0) & (src >= 0) & (src < 32)
            key = win[j][rs // 2, fi, rs % 2]
            key = jnp.where(ok, key, jnp.zeros_like(key))
            key = jnp.dot(back[...], key, preferred_element_type=F32).astype(BF16)
            if n:
                cut = W - 16 * turn
                kbuf[ro, W + 16 * turn : 2 * W, :] = key[0:cut]
                kbuf[ro, W : W + 16 * turn, :] = key[cut:W]
            else:
                kbuf[ro, 0:W, :] = key
        m = lax.dot_general(qm[ro], kbuf[ro], NT, preferred_element_type=F32)
        for g in range(G):
            rows = m[g * W : (g + 1) * W].astype(BF16)
            both = rows[:, 0:W] * band[p, 0] + rows[:, W : 2 * W] * band[p, 1]
            skew[ro, g * W : (g + 1) * W, p * W : (p + 1) * W] = pltpu.roll(
                both, 0, 1, stride=1, stride_axis=0
            )
        return c

    lax.fori_loop(0, NROWS, one, 0, unroll=True)


def finish(row, tgt, occ, grad, t1, t2, pick, skew, pad, x3, hid):
    lane = iota((W, W), 1)
    top = 4 * (row // 2)

    def cost_row(ro, c):
        src = top - 2 + ro
        live = (src >= 0) & (src < 32)
        for h in range(2):
            picked = [
                jnp.dot(
                    skew[ro, (4 * h + gq) * W : (4 * h + gq + 1) * W, :],
                    pick[gq],
                    preferred_element_type=F32,
                )
                for gq in range(4)
            ]
            for j in range(TILES):
                x = picked[0]
                for gq in range(1, 4):
                    x = jnp.where(lane // 32 == (j + gq) % 4, picked[gq], x)
                s = 2 * j + h
                pad[s, 8 : 8 + W, :] = jnp.where(live, x * SCALE, 0.0)
                for e in range(3):
                    at = e * 256 + h * W
                    x3[j, ro, :, at : at + W] = pad[s, 7 + e : 7 + e + W, :].astype(BF16)
        return c

    lax.fori_loop(0, NROWS, cost_row, 0, unroll=2)

    def tile(j, c):
        total = jnp.dot(x3[j, 0:6].reshape(6 * W, 768), t1[j, 0], preferred_element_type=F32)
        for b in (1, 2):
            total += jnp.dot(x3[j, b : b + 6].reshape(6 * W, 768), t1[j, b], preferred_element_type=F32)
        d = STEP * j - 1 + iota((W, 256), 1) % 32
        inside = (d >= 0) & (d < D)
        for h in range(6):
            src = top - 1 + h
            ok = inside & ((src >= 0) & (src < 32))
            hid[h] = jnp.where(ok, jnp.maximum(total[h * W : (h + 1) * W], 0.0), 0.0).astype(BF16)
        out = jnp.zeros((96, 512), F32)
        for b in range(3):
            out += lax.dot_general(t2[b], hid[b : b + 4].reshape(512, 256), NT, preferred_element_type=F32)
        for r in range(4):
            cut = out[:, r * W : (r + 1) * W]
            wl = iota((STEP, W), 1)
            logits = (
                cut[32 : 32 + STEP]
                + jnp.where(wl == 0, 0.0, pltpu.roll(cut[0:STEP], 1, 1))
                + jnp.where(wl == W - 1, 0.0, pltpu.roll(cut[64 : 64 + STEP], W - 1, 1))
            )
            sig = jax.nn.sigmoid(logits)
            ds = pl.ds(j * STEP, STEP)
            occ[r // 2, ds, r % 2, :] = sig.astype(BF16)
            hits = tgt[D : D + 1, r * W : (r + 1) * W]
            spots = tgt[pl.ds(pl.multiple_of(j * STEP, 8), STEP), r * W : (r + 1) * W]
            grad[r // 2, ds, r % 2, :] = hits * sig - spots
        return c

    lax.fori_loop(0, TILES, tile, 0)


MESH = pl.DeviceIdType.MESH
REACH = 4
ORDER = (0, 1, 4, 3, 2)
EDGE = (1, 3, 4)


def fused_kernel(*refs):
    feat, pts, shift, first_ref, last_ref, occ, grad = refs[:7]
    win = refs[7 : 8 + REACH]
    rest = refs[8 + REACH :]
    allpts, v1, v2, t1, t2, band, pick, back, qm, kbuf, skew, pad, x3, hid, tgt = rest[:15]
    occ_out, grad_out, send, recv, relay_send, psend, precv, own, esend, osend, orecv = rest[15:]
    f = lax.axis_index("frame")
    r = lax.axis_index("row")
    frames = lax.axis_size("frame")
    rows = lax.axis_size("row")
    core = r % 2
    sibling = r + 1 - 2 * core
    center = 2 + core

    def inside(there):
        return (there >= 0) & (there < rows)

    def crosses(off):
        return inside(r + off) & ((r + off) // (rows // 2) != r // (rows // 2))

    def by_frames(j, there):
        if j not in EDGE:
            return False
        if j == 4:
            return True
        return (there - j) // (frames // 2) == there // (frames // 2)

    barrier = pltpu.get_barrier_semaphore()

    def greet(there_f, there_r):
        pl.semaphore_signal(
            barrier, inc=1, device_id={"frame": there_f, "row": there_r}, device_id_type=MESH
        )

    for off in range(1, rows):
        greet(f, (r + off) % rows)
    for j in range(1, REACH + 1):
        pl.when(f + j < frames)(lambda j=j: greet(f + j, r))
        pl.when(f - j >= 0)(lambda j=j: greet(f - j, r))
    later = jnp.minimum(frames - 1 - f, REACH)
    earlier = jnp.minimum(f, REACH)
    pl.semaphore_wait(barrier, rows - 1 + later + earlier)

    def frame_copy(j, there):
        return pltpu.make_async_remote_copy(
            src_ref=feat,
            dst_ref=win[j].at[center],
            send_sem=send.at[0, j],
            recv_sem=recv.at[center, j],
            device_id={"frame": there, "row": r},
            device_id_type=MESH,
        )

    def row_copy(lane, j, q, there):
        return pltpu.make_async_remote_copy(
            src_ref=feat if j == 0 else win[j].at[center],
            dst_ref=win[j].at[q],
            send_sem=send.at[lane, j],
            recv_sem=recv.at[q, j],
            device_id={"frame": f, "row": there},
            device_id_type=MESH,
        )

    def relay_copy(n, j, q):
        return pltpu.make_async_remote_copy(
            src_ref=win[j].at[q],
            dst_ref=win[j].at[q],
            send_sem=relay_send.at[n, j],
            recv_sem=recv.at[q, j],
            device_id={"frame": f, "row": sibling},
            device_id_type=MESH,
        )

    def point_copy(off):
        there = (r + off) % rows
        return pltpu.make_async_remote_copy(
            src_ref=pts,
            dst_ref=allpts.at[r],
            send_sem=psend.at[off],
            recv_sem=precv.at[r],
            device_id={"frame": f, "row": there},
            device_id_type=MESH,
        )

    def point_arrival(off):
        there = (r + off) % rows
        return pltpu.make_async_remote_copy(
            src_ref=pts,
            dst_ref=allpts.at[there],
            send_sem=psend.at[off],
            recv_sem=precv.at[there],
            device_id={"frame": f, "row": there},
            device_id_type=MESH,
        )

    def row_sends(j, act):
        for lane, q, off in ((2, core, 2), (3, 4 + core, -2)):
            ok = inside(r + off) & (f >= j)
            if j in EDGE:
                ok = ok & jnp.logical_not(crosses(off) & by_frames(j, f))
            pl.when(ok)(lambda lane=lane, q=q, off=off: act(row_copy(lane, j, q, r + off)))
        pl.when(f >= j)(lambda: act(row_copy(1, j, center, sibling)))

    def edge_sends(act):
        for n, (q, off) in enumerate(((core, -2), (4 + core, 2))):
            for j in EDGE:
                copy = pltpu.make_async_remote_copy(
                    src_ref=win[0].at[q],
                    dst_ref=win[j].at[q],
                    send_sem=esend.at[n, j],
                    recv_sem=recv.at[q, j],
                    device_id={"frame": f + j, "row": r},
                    device_id_type=MESH,
                )
                ok = crosses(off) & (f + j < frames) & by_frames(j, f + j)
                pl.when(ok)(lambda copy=copy: act(copy))

    def relay(j, act, wait_first):
        for n, (q, off) in enumerate(((core, -2), (4 + core, 2))):

            def body(n=n, q=q):
                copy = relay_copy(n, j, q)
                if wait_first:
                    copy.wait_recv()
                act(copy)

            pl.when(inside(r + off) & (f >= j))(body)

    def start(copy):
        copy.start()

    def arrive(j):
        pl.when(f >= j)(lambda: row_copy(1, j, 5 - center, sibling).wait_recv())
        for q, off in ((1 - core, -2), (5 - core, 2)):
            ok = inside(r + off) & (f >= j)
            pl.when(ok)(lambda q=q: row_copy(1, j, q, sibling).wait_recv())

    def step(j):
        pl.when(f >= j)(lambda: frame_copy(j, f).wait_recv())
        row_sends(j, start)

    def count(part):
        counts = count_points(allpts, core, r, part * (rows // 4), rows // 4)
        for half in range(2):
            tgt[:, half * 256 : half * 256 + 256] += counts[half]

    def scores(slot, p):
        score(slot, p, f, r, shift, win, band, back, qm, kbuf, skew)

    mine = pltpu.make_async_copy(feat, win[0].at[center], own.at[0])
    mine_pts = pltpu.make_async_copy(pts, allpts.at[r], own.at[1])
    for off in range(1, rows):
        point_copy(off).start()
    mine.start()
    mine_pts.start()
    row_sends(0, start)
    for j in (1, 4, 3, 2):
        pl.when(f + j < frames)(lambda j=j: frame_copy(j, f + j).start())
    build_tables(first_ref, last_ref, v1, v2, t1, t2, band, pick, back)
    for s in range(2 * TILES):
        pad[s, 0:8, :] = jnp.zeros((8, W), F32)
        pad[s, 136:144, :] = jnp.zeros((8, W), F32)
    tgt[...] = jnp.zeros_like(tgt)
    step(1)
    step(4)
    relay(0, start, True)
    edge_sends(start)
    for off in range(1, rows):
        point_arrival(off).wait_recv()
    mine.wait()
    mine_pts.wait()
    count(0)
    step(3)
    step(2)
    relay(1, start, True)
    count(1)
    relay(4, start, True)
    count(2)
    arrive(0)
    build_queries(core, win[0], qm)
    relay(3, start, True)
    count(3)
    arrive(1)
    arrive(4)

    @pl.when(core == 0)
    def _():
        scores(0, 0)
        scores(0, 1)

    @pl.when(core == 1)
    def _():
        scores(1, 0)

    relay(2, start, True)
    arrive(3)

    @pl.when(core == 1)
    def _():
        scores(1, 1)
        scores(1, 2)

    arrive(2)

    @pl.when(core == 0)
    def _():
        scores(0, 2)
        scores(0, 3)

    @pl.when(core == 1)
    def _():
        scores(1, 3)

    finish(r, tgt, occ_out, grad_out, t1, t2, pick, skew, pad, x3, hid)

    def swap(n, src, dst):
        return pltpu.make_async_remote_copy(
            src_ref=src.at[1 - core],
            dst_ref=dst.at[core],
            send_sem=osend.at[n],
            recv_sem=orecv.at[n],
            device_id={"frame": f, "row": sibling},
            device_id_type=MESH,
        )

    swaps = (swap(0, occ_out, occ), swap(1, grad_out, grad))
    keeps = (
        pltpu.make_async_copy(occ_out.at[core], occ.at[core], own.at[2]),
        pltpu.make_async_copy(grad_out.at[core], grad.at[core], own.at[3]),
    )
    for copy in swaps + keeps:
        copy.start()
    for j in range(1, REACH + 1):
        pl.when(f + j < frames)(lambda j=j: frame_copy(j, f + j).wait_send())
    edge_sends(lambda copy: copy.wait_send())
    for j in ORDER:
        row_sends(j, lambda copy: copy.wait_send())
        relay(j, lambda copy: copy.wait_send(), False)
    for off in range(1, rows):
        point_copy(off).wait_send()
    for copy in swaps + keeps:
        copy.wait()


def settle_kernel(occ, grad, occ_out, grad_out):
    occ_out[...] = occ[...]
    grad_out[...] = grad[...]


def settle(occ, grad):
    block = pl.BlockSpec((1, D, 2, W), lambda s: (s, 0, 0, 0))
    return pl.pallas_call(
        settle_kernel,
        grid=(2,),
        out_shape=(
            jax.ShapeDtypeStruct(occ.shape, occ.dtype),
            jax.ShapeDtypeStruct(grad.shape, grad.dtype),
        ),
        in_specs=[block, block],
        out_specs=(block, block),
        name="settle",
    )(occ, grad)


def shards(features, row_shift, lidar_points, conv_first, conv_last):
    points = jnp.transpose(lidar_points, (1, 0, 2)).astype(BF16)
    first = jnp.transpose(conv_first, (2, 3, 4, 0, 1))
    last = jnp.transpose(conv_last[0], (1, 2, 3, 0))
    count = lax.axis_size("row")
    vmem = pl.BlockSpec(memory_space=pltpu.VMEM)
    smem = pl.BlockSpec(memory_space=pltpu.SMEM)
    hbm = pl.BlockSpec(memory_space=pl.ANY)
    dma = pltpu.SemaphoreType.DMA
    both = pl.pallas_call(
        fused_kernel,
        out_shape=(
            jax.ShapeDtypeStruct((2, D, 2, W), BF16),
            jax.ShapeDtypeStruct((2, D, 2, W), F32),
        ),
        in_specs=[vmem, vmem, smem, vmem, vmem],
        out_specs=(hbm, hbm),
        scratch_shapes=[pltpu.VMEM((6,) + features.shape, BF16) for _ in range(REACH + 1)]
        + [
            pltpu.VMEM((count,) + points.shape, BF16),
            pltpu.VMEM((27, G, 256), F32),
            pltpu.VMEM((9, 3, 256), F32),
            pltpu.VMEM((TILES, 3, 768, 256), BF16),
            pltpu.VMEM((3, 96, 256), BF16),
            pltpu.VMEM((4, 2, W, W), BF16),
            pltpu.VMEM((4, 4 * W, W), BF16),
            pltpu.VMEM((W, W), BF16),
            pltpu.VMEM((NROWS, G * W, W), BF16),
            pltpu.VMEM((NROWS, 2 * W, W), BF16),
            pltpu.VMEM((NROWS, G * W, 4 * W), BF16),
            pltpu.VMEM((2 * TILES, 144, W), F32),
            pltpu.VMEM((TILES, NROWS, W, 768), BF16),
            pltpu.VMEM((6, W, 256), BF16),
            pltpu.VMEM((104, 512), F32),
            pltpu.VMEM((2, D, 2, W), BF16),
            pltpu.VMEM((2, D, 2, W), F32),
            dma((4, REACH + 1)),
            dma((6, REACH + 1)),
            dma((2, REACH + 1)),
            dma((count,)),
            dma((count,)),
            dma((4,)),
            dma((2, REACH + 1)),
            dma((2,)),
            dma((2,)),
        ],
        compiler_params=pltpu.CompilerParams(
            collective_id=0, has_side_effects=True, vmem_limit_bytes=60000 * 1024
        ),
        name="fused_volume",
    )(features, points, row_shift.T, first, last)
    return settle(*both)


def solution(mesh):
    P = jax.sharding.PartitionSpec
    out = P("frame", None, "row", None)
    return jax.shard_map(
        shards,
        mesh=mesh,
        in_specs=(P("frame", "row", None, None), P(), P("frame", None, "row"), P(), P()),
        out_specs=(out, out),
        check_vma=False,
    )
```

```python
import functools
import math

import jax
import jax.numpy as jnp
from jax import lax
from jax.experimental import pallas as pl
from jax.experimental.pallas import tpu as pltpu

G = 8
D = 96
HIST = 8
W = 128
TILES = 4
STEP = D // TILES
NROWS = 8
F32, BF16, I32 = jnp.float32, jnp.bfloat16, jnp.int32
NT = (((1,), (1,)), ((), ()))
PAIRS = ((8, 2, 6), (7, 1, 6), (6, 3, 5), (5, 4, 4))
SCALE = 1.0 / math.sqrt(HIST * 16)


def iota(shape, dim):
    return lax.broadcasted_iota(I32, shape, dim)


def build_tables(first_ref, last_ref, v1, v2, t1, t2, band, pick, back):
    grow = jnp.where(iota((G, 256), 1) // 32 == iota((G, 256), 0), 1.0, 0.0).astype(BF16)
    tn = (((0,), (0,)), ((), ()))
    for a in range(3):
        for b in range(3):
            for e in range(3):
                w = first_ref[a, b, e]
                v1[(a * 3 + b) * 3 + e] = lax.dot_general(w, grow, tn, preferred_element_type=F32)
            v2[a * 3 + b] = jnp.dot(last_ref[a, b], grow, preferred_element_type=F32)
    m = iota((32, 256), 1) % 32
    li = iota((32, 256), 0)
    masks = [(li == m + a) & (m < STEP + 2) for a in range(3)]

    def first(b, c):
        for e in range(3):
            for i in range(G):
                block = jnp.zeros((32, 256), F32)
                for a in range(3):
                    row = v1[a * 9 + e + 3 * b, i : i + 1, :]
                    block = jnp.where(masks[a], row, block)
                at = (e * G + i) * 32
                t1[0, b, at : at + 32, :] = block.astype(BF16)
        return c

    lax.fori_loop(0, 3, first, 0)
    rows2 = [(m == li + a) & (li < STEP) for a in range(3)]

    def last(b, c):
        for e in range(3):
            block = jnp.zeros((32, 256), F32)
            for a in range(3):
                row = v2[a * 3 + b, e : e + 1, :]
                block = jnp.where(rows2[a], row, block)
            t2[b, e * 32 : e * 32 + 32, :] = block.astype(BF16)
        return c

    lax.fori_loop(0, 3, last, 0)

    lane = iota((W, W), 1)
    w = iota((W, W), 0)
    for p, (ka, kb, turn) in enumerate(PAIRS):
        for n, (k, base) in enumerate(((ka, 0), (kb, 16 * turn))):
            s = (lane + w + 1 - base) & (W - 1)
            ok = (s < 12 * k) & (s <= w)
            band[p, n] = jnp.where(ok, 1.0, 0.0).astype(BF16)
    for gq in range(4):
        low = lane % 32
        d = STEP * ((lane // 32 - gq + 4) % 4) - 2 + low
        real = (low < STEP + 4) & (d >= 0) & (d < D)
        for p, (ka, kb, turn) in enumerate(PAIRS):
            hit = (w == (((d * ka) >> 3) + W - 1) % W) | (w == (((d * kb) >> 3) + 16 * turn - 1) % W)
            pick[gq, p * W : (p + 1) * W, :] = jnp.where(hit & real, 1.0, 0.0).astype(BF16)
    back[...] = jnp.where(lane + w == W - 1, 1.0, 0.0).astype(BF16)

    def turned(b, c):
        for j in range(1, TILES):
            for e in range(3):
                for h in range(2):
                    for q in range(4):
                        at = e * 256 + h * W
                        t1[j, b, at + q * 32 : at + q * 32 + 32, :] = t1[
                            0, b, at + ((q - j) % 4) * 32 : at + ((q - j) % 4) * 32 + 32, :
                        ]
        return c

    lax.fori_loop(0, 3, turned, 0)


def count_points(pts, slot, row, begin, count):
    n = pts.shape[3]
    one = jnp.ones((), BF16)
    zero = jnp.zeros((), BF16)
    bins = iota((104, n), 0)
    spots = iota((256, n), 0).astype(BF16)

    def points(src, totals):
        both = [pts[src, c].astype(F32) for c in range(3)]
        p = [jnp.where(slot == 0, x[0:1], x[1:2]) for x in both]
        left = jnp.where((bins.astype(BF16) == p[2].astype(BF16)) | (bins >= D), one, zero)
        added = []
        for half in range(2):
            local = p[0] - (4 * (row // 2) + 2 * half).astype(F32)
            inside = (local >= 0) & (local < 2)
            code = jnp.where(inside, local * W + p[1], -1.0).astype(BF16)
            right = jnp.where(spots == code, one, zero)
            added.append(
                totals[half] + lax.dot_general(left, right, NT, preferred_element_type=F32)
            )
        return tuple(added)

    nothing = jnp.zeros((104, 256), F32)
    return lax.fori_loop(begin, begin + count, points, (nothing, nothing), unroll=2)


def build_queries(core, win0, qm):
    lane = iota((W, W), 1)

    def one(ro, c):
        rr = ro + 2
        q = win0[rr // 2, core, rr % 2]
        for g in range(G):
            qm[ro, g * W : (g + 1) * W, :] = jnp.where(lane // 16 == g, q, jnp.zeros_like(q))
        return c

    lax.fori_loop(0, NROWS, one, 0)


def score(slot, p, frame, row, shift, win, band, back, qm, kbuf, skew):
    t = 2 * frame + slot
    ka, kb, turn = PAIRS[p]

    def one(ro, c):
        for n, k in enumerate((ka, kb)):
            j = (k - slot + 1) // 2
            fi = slot - k + 2 * j
            rs = ro + 2 + shift[k - 1, t]
            src = 4 * (row // 2) - 4 + rs
            ok = (t - k >= 0) & (src >= 0) & (src < 32)
            key = win[j][rs // 2, fi, rs % 2]
            key = jnp.where(ok, key, jnp.zeros_like(key))
            key = jnp.dot(back[...], key, preferred_element_type=F32).astype(BF16)
            if n:
                cut = W - 16 * turn
                kbuf[ro, W + 16 * turn : 2 * W, :] = key[0:cut]
                kbuf[ro, W : W + 16 * turn, :] = key[cut:W]
            else:
                kbuf[ro, 0:W, :] = key
        m = lax.dot_general(qm[ro], kbuf[ro], NT, preferred_element_type=F32)
        for g in range(G):
            rows = m[g * W : (g + 1) * W].astype(BF16)
            both = rows[:, 0:W] * band[p, 0] + rows[:, W : 2 * W] * band[p, 1]
            skew[ro, g * W : (g + 1) * W, p * W : (p + 1) * W] = pltpu.roll(
                both, 0, 1, stride=1, stride_axis=0
            )
        return c

    lax.fori_loop(0, NROWS, one, 0, unroll=True)


def finish(row, tgt, occ, grad, t1, t2, pick, skew, pad, x3, hid):
    lane = iota((W, W), 1)
    top = 4 * (row // 2)

    def cost_row(ro, c):
        src = top - 2 + ro
        live = (src >= 0) & (src < 32)
        for h in range(2):
            picked = [
                jnp.dot(
                    skew[ro, (4 * h + gq) * W : (4 * h + gq + 1) * W, :],
                    pick[gq],
                    preferred_element_type=F32,
                )
                for gq in range(4)
            ]
            for j in range(TILES):
                x = picked[0]
                for gq in range(1, 4):
                    x = jnp.where(lane // 32 == (j + gq) % 4, picked[gq], x)
                s = 2 * j + h
                pad[s, 8 : 8 + W, :] = jnp.where(live, x * SCALE, 0.0)
                for e in range(3):
                    at = e * 256 + h * W
                    x3[j, ro, :, at : at + W] = pad[s, 7 + e : 7 + e + W, :].astype(BF16)
        return c

    lax.fori_loop(0, NROWS, cost_row, 0, unroll=2)

    def tile(j, c):
        total = jnp.dot(x3[j, 0:6].reshape(6 * W, 768), t1[j, 0], preferred_element_type=F32)
        for b in (1, 2):
            total += jnp.dot(x3[j, b : b + 6].reshape(6 * W, 768), t1[j, b], preferred_element_type=F32)
        d = STEP * j - 1 + iota((W, 256), 1) % 32
        inside = (d >= 0) & (d < D)
        for h in range(6):
            src = top - 1 + h
            ok = inside & ((src >= 0) & (src < 32))
            hid[h] = jnp.where(ok, jnp.maximum(total[h * W : (h + 1) * W], 0.0), 0.0).astype(BF16)
        out = jnp.zeros((96, 512), F32)
        for b in range(3):
            out += lax.dot_general(t2[b], hid[b : b + 4].reshape(512, 256), NT, preferred_element_type=F32)
        for r in range(4):
            cut = out[:, r * W : (r + 1) * W]
            wl = iota((STEP, W), 1)
            logits = (
                cut[32 : 32 + STEP]
                + jnp.where(wl == 0, 0.0, pltpu.roll(cut[0:STEP], 1, 1))
                + jnp.where(wl == W - 1, 0.0, pltpu.roll(cut[64 : 64 + STEP], W - 1, 1))
            )
            sig = jax.nn.sigmoid(logits)
            ds = pl.ds(j * STEP, STEP)
            occ[r // 2, ds, r % 2, :] = sig.astype(BF16)
            hits = tgt[D : D + 1, r * W : (r + 1) * W]
            spots = tgt[pl.ds(pl.multiple_of(j * STEP, 8), STEP), r * W : (r + 1) * W]
            grad[r // 2, ds, r % 2, :] = hits * sig - spots
        return c

    lax.fori_loop(0, TILES, tile, 0)


MESH = pl.DeviceIdType.MESH
REACH = 4
ORDER = (0, 1, 4, 3, 2)
EDGE = (1, 3, 4)


def fused_kernel(*refs):
    feat, pts, shift, first_ref, last_ref, occ, grad = refs[:7]
    win = refs[7 : 8 + REACH]
    rest = refs[8 + REACH :]
    allpts, detour, v1, v2, t1, t2, band, pick, back, qm, kbuf, skew, pad, x3, hid, tgt = rest[:16]
    occ_out, grad_out, send, recv, relay_send, psend, precv, own, esend, osend, orecv, dsem = rest[16:]
    f = lax.axis_index("frame")
    r = lax.axis_index("row")
    frames = lax.axis_size("frame")
    rows = lax.axis_size("row")
    core = r % 2
    sibling = r + 1 - 2 * core
    center = 2 + core

    def inside(there):
        return (there >= 0) & (there < rows)

    def crosses(off):
        return inside(r + off) & ((r + off) // (rows // 2) != r // (rows // 2))

    mid = frames // 2

    def by_frames(j, there, off):
        near = (there - j) // mid == there // mid
        edge = {1: near, 3: near | (there == mid), 4: True}.get(j, False)
        inner = {4: (there == mid) | (there == mid + 1), 3: (there == frames - 1) | (there == mid - 1)}.get(j, False)
        return (crosses(off) & edge) | (jnp.logical_not(crosses(off)) & inner)

    barrier = pltpu.get_barrier_semaphore()

    def greet(there_f, there_r):
        pl.semaphore_signal(
            barrier, inc=1, device_id={"frame": there_f, "row": there_r}, device_id_type=MESH
        )

    for off in range(2, rows, 2):
        greet(f, (r + off) % rows)
    greet(f, sibling)
    for j in range(1, REACH + 1):
        pl.when(f + j < frames)(lambda j=j: greet(f + j, r))
        pl.when(f - j >= 0)(lambda j=j: greet(f - j, r))
    later = jnp.minimum(frames - 1 - f, REACH)
    earlier = jnp.minimum(f, REACH)
    pl.semaphore_wait(barrier, rows // 2 + later + earlier)

    def frame_copy(j, there):
        return pltpu.make_async_remote_copy(
            src_ref=feat,
            dst_ref=win[j].at[center],
            send_sem=send.at[0, j],
            recv_sem=recv.at[center, j],
            device_id={"frame": there, "row": r},
            device_id_type=MESH,
        )

    def detour_copy():
        return pltpu.make_async_remote_copy(
            src_ref=feat,
            dst_ref=detour,
            send_sem=dsem.at[0],
            recv_sem=dsem.at[1],
            device_id={"frame": 0, "row": r},
            device_id_type=MESH,
        )

    def onward_copy():
        return pltpu.make_async_remote_copy(
            src_ref=detour,
            dst_ref=win[1].at[center],
            send_sem=dsem.at[2],
            recv_sem=recv.at[center, 1],
            device_id={"frame": mid, "row": r},
            device_id_type=MESH,
        )

    def direct(j):
        return (f + j < frames) & ((j != 1) | (f != mid - 1))

    def row_copy(lane, j, q, there):
        return pltpu.make_async_remote_copy(
            src_ref=feat if j == 0 else win[j].at[center],
            dst_ref=win[j].at[q],
            send_sem=send.at[lane, j],
            recv_sem=recv.at[q, j],
            device_id={"frame": f, "row": there},
            device_id_type=MESH,
        )

    def relay_copy(n, j, q):
        return pltpu.make_async_remote_copy(
            src_ref=win[j].at[q],
            dst_ref=win[j].at[q],
            send_sem=relay_send.at[n, j],
            recv_sem=recv.at[q, j],
            device_id={"frame": f, "row": sibling},
            device_id_type=MESH,
        )

    def point_copy(n, src, slot, there):
        return pltpu.make_async_remote_copy(
            src_ref=src,
            dst_ref=allpts.at[slot],
            send_sem=psend.at[n],
            recv_sem=precv.at[slot],
            device_id={"frame": f, "row": there},
            device_id_type=MESH,
        )

    def points_out(act):
        act(point_copy(1, pts, r, sibling))
        for off in range(2, rows, 2):
            act(point_copy(off, pts, r, (r + off) % rows))

    def points_on(act, wait_first):
        for off in range(2, rows, 2):
            there = (r + off) % rows
            if wait_first:
                point_copy(off, pts, there, sibling).wait_recv()
            act(point_copy(off + 1, allpts.at[there], there, sibling))

    def row_sends(j, act):
        for lane, q, off in ((2, core, 2), (3, 4 + core, -2)):
            ok = inside(r + off) & (f >= j)
            if j in EDGE:
                ok = ok & jnp.logical_not(by_frames(j, f, off))
            pl.when(ok)(lambda lane=lane, q=q, off=off: act(row_copy(lane, j, q, r + off)))
        pl.when(f >= j)(lambda: act(row_copy(1, j, center, sibling)))

    def edge_sends(act):
        for n, (q, off) in enumerate(((core, -2), (4 + core, 2))):
            for j in EDGE:
                copy = pltpu.make_async_remote_copy(
                    src_ref=win[0].at[q],
                    dst_ref=win[j].at[q],
                    send_sem=esend.at[n, j],
                    recv_sem=recv.at[q, j],
                    device_id={"frame": f + j, "row": r},
                    device_id_type=MESH,
                )
                ok = inside(r + off) & (f + j < frames) & by_frames(j, f + j, off)
                pl.when(ok)(lambda copy=copy: act(copy))

    def relay(j, act, wait_first):
        for n, (q, off) in enumerate(((core, -2), (4 + core, 2))):

            def body(n=n, q=q):
                copy = relay_copy(n, j, q)
                if wait_first:
                    copy.wait_recv()
                act(copy)

            pl.when(inside(r + off) & (f >= j))(body)

    def start(copy):
        copy.start()

    def arrive(j):
        pl.when(f >= j)(lambda: row_copy(1, j, 5 - center, sibling).wait_recv())
        for q, off in ((1 - core, -2), (5 - core, 2)):
            ok = inside(r + off) & (f >= j)
            pl.when(ok)(lambda q=q: row_copy(1, j, q, sibling).wait_recv())

    def step(j):
        pl.when(f >= j)(lambda: frame_copy(j, f).wait_recv())
        row_sends(j, start)

    def count(part):
        counts = count_points(allpts, core, r, part * (rows // 4), rows // 4)
        for half in range(2):
            tgt[:, half * 256 : half * 256 + 256] += counts[half]

    def scores(slot, p):
        score(slot, p, f, r, shift, win, band, back, qm, kbuf, skew)

    mine = pltpu.make_async_copy(feat, win[0].at[center], own.at[0])
    mine_pts = pltpu.make_async_copy(pts, allpts.at[r], own.at[1])
    points_out(start)
    mine.start()
    mine_pts.start()
    row_sends(0, start)
    pl.when(f == mid - 1)(lambda: detour_copy().start())
    for j in (1, 4, 3, 2):
        pl.when(direct(j))(lambda j=j: frame_copy(j, f + j).start())
    build_tables(first_ref, last_ref, v1, v2, t1, t2, band, pick, back)

    @pl.when(f == 0)
    def _():
        detour_copy().wait_recv()
        onward_copy().start()

    for s in range(2 * TILES):
        pad[s, 0:8, :] = jnp.zeros((8, W), F32)
        pad[s, 136:144, :] = jnp.zeros((8, W), F32)
    tgt[...] = jnp.zeros_like(tgt)
    step(1)
    step(4)
    points_on(start, True)
    relay(0, start, True)
    edge_sends(start)
    point_copy(1, pts, sibling, sibling).wait_recv()
    for off in range(2, rows, 2):
        point_copy(off, pts, (sibling + off) % rows, sibling).wait_recv()
    mine.wait()
    mine_pts.wait()
    count(0)
    step(3)
    step(2)
    relay(1, start, True)
    count(1)
    relay(4, start, True)
    count(2)
    arrive(0)
    build_queries(core, win[0], qm)
    relay(3, start, True)
    count(3)
    arrive(1)
    arrive(4)

    @pl.when(core == 0)
    def _():
        scores(0, 0)
        scores(0, 1)

    @pl.when(core == 1)
    def _():
        scores(1, 0)

    relay(2, start, True)
    arrive(3)

    @pl.when(core == 1)
    def _():
        scores(1, 1)
        scores(1, 2)

    arrive(2)

    @pl.when(core == 0)
    def _():
        scores(0, 2)
        scores(0, 3)

    @pl.when(core == 1)
    def _():
        scores(1, 3)

    finish(r, tgt, occ_out, grad_out, t1, t2, pick, skew, pad, x3, hid)

    def swap(n, src, dst):
        return pltpu.make_async_remote_copy(
            src_ref=src.at[1 - core],
            dst_ref=dst.at[core],
            send_sem=osend.at[n],
            recv_sem=orecv.at[n],
            device_id={"frame": f, "row": sibling},
            device_id_type=MESH,
        )

    swaps = (swap(0, occ_out, occ), swap(1, grad_out, grad))
    keeps = (
        pltpu.make_async_copy(occ_out.at[core], occ.at[core], own.at[2]),
        pltpu.make_async_copy(grad_out.at[core], grad.at[core], own.at[3]),
    )
    for copy in swaps + keeps:
        copy.start()
    for j in range(1, REACH + 1):
        pl.when(direct(j))(lambda j=j: frame_copy(j, f + j).wait_send())
    pl.when(f == mid - 1)(lambda: detour_copy().wait_send())
    pl.when(f == 0)(lambda: onward_copy().wait_send())
    edge_sends(lambda copy: copy.wait_send())
    for j in ORDER:
        row_sends(j, lambda copy: copy.wait_send())
        relay(j, lambda copy: copy.wait_send(), False)
    points_out(lambda copy: copy.wait_send())
    points_on(lambda copy: copy.wait_send(), False)
    for copy in swaps + keeps:
        copy.wait()


def settle_kernel(occ, grad, occ_out, grad_out):
    occ_out[...] = occ[...]
    grad_out[...] = grad[...]


def settle(occ, grad):
    block = pl.BlockSpec((1, D, 2, W), lambda s: (s, 0, 0, 0))
    return pl.pallas_call(
        settle_kernel,
        grid=(2,),
        out_shape=(
            jax.ShapeDtypeStruct(occ.shape, occ.dtype),
            jax.ShapeDtypeStruct(grad.shape, grad.dtype),
        ),
        in_specs=[block, block],
        out_specs=(block, block),
        name="settle",
    )(occ, grad)


def shards(features, row_shift, lidar_points, conv_first, conv_last):
    points = jnp.transpose(lidar_points, (1, 0, 2))
    first = jnp.transpose(conv_first, (2, 3, 4, 0, 1))
    last = jnp.transpose(conv_last[0], (1, 2, 3, 0))
    count = lax.axis_size("row")
    vmem = pl.BlockSpec(memory_space=pltpu.VMEM)
    smem = pl.BlockSpec(memory_space=pltpu.SMEM)
    hbm = pl.BlockSpec(memory_space=pl.ANY)
    dma = pltpu.SemaphoreType.DMA
    both = pl.pallas_call(
        fused_kernel,
        out_shape=(
            jax.ShapeDtypeStruct((2, D, 2, W), BF16),
            jax.ShapeDtypeStruct((2, D, 2, W), F32),
        ),
        in_specs=[vmem, vmem, smem, vmem, vmem],
        out_specs=(hbm, hbm),
        scratch_shapes=[pltpu.VMEM((6,) + features.shape, BF16) for _ in range(REACH + 1)]
        + [
            pltpu.VMEM((count,) + points.shape, I32),
            pltpu.VMEM(features.shape, BF16),
            pltpu.VMEM((27, G, 256), F32),
            pltpu.VMEM((9, 3, 256), F32),
            pltpu.VMEM((TILES, 3, 768, 256), BF16),
            pltpu.VMEM((3, 96, 256), BF16),
            pltpu.VMEM((4, 2, W, W), BF16),
            pltpu.VMEM((4, 4 * W, W), BF16),
            pltpu.VMEM((W, W), BF16),
            pltpu.VMEM((NROWS, G * W, W), BF16),
            pltpu.VMEM((NROWS, 2 * W, W), BF16),
            pltpu.VMEM((NROWS, G * W, 4 * W), BF16),
            pltpu.VMEM((2 * TILES, 144, W), F32),
            pltpu.VMEM((TILES, NROWS, W, 768), BF16),
            pltpu.VMEM((6, W, 256), BF16),
            pltpu.VMEM((104, 512), F32),
            pltpu.VMEM((2, D, 2, W), BF16),
            pltpu.VMEM((2, D, 2, W), F32),
            dma((4, REACH + 1)),
            dma((6, REACH + 1)),
            dma((2, REACH + 1)),
            dma((count,)),
            dma((count,)),
            dma((4,)),
            dma((2, REACH + 1)),
            dma((2,)),
            dma((2,)),
            dma((3,)),
        ],
        compiler_params=pltpu.CompilerParams(
            collective_id=0, has_side_effects=True, vmem_limit_bytes=60000 * 1024
        ),
        name="fused_volume",
    )(features, points, row_shift.T, first, last)
    return settle(*both)


def solution(mesh):
    P = jax.sharding.PartitionSpec
    out = P("frame", None, "row", None)
    return jax.shard_map(
        shards,
        mesh=mesh,
        in_specs=(P("frame", "row", None, None), P(), P("frame", None, "row"), P(), P()),
        out_specs=(out, out),
        check_vma=False,
    )
```

```python
import functools
import math

import jax
import jax.numpy as jnp
from jax import lax
from jax.experimental import pallas as pl
from jax.experimental.pallas import tpu as pltpu

G = 8
D = 96
HIST = 8
W = 128
TILES = 4
STEP = D // TILES
NROWS = 8
F32, BF16, I32 = jnp.float32, jnp.bfloat16, jnp.int32
NT = (((1,), (1,)), ((), ()))
PAIRS = ((8, 2, 6), (7, 1, 6), (6, 3, 5), (5, 4, 4))
SCALE = 1.0 / math.sqrt(HIST * 16)


def iota(shape, dim):
    return lax.broadcasted_iota(I32, shape, dim)


def build_tables(first_ref, last_ref, v1, v2, t1, t2, band, pick, back):
    grow = jnp.where(iota((G, 256), 1) // 32 == iota((G, 256), 0), 1.0, 0.0).astype(BF16)
    tn = (((0,), (0,)), ((), ()))
    for a in range(3):
        for b in range(3):
            for e in range(3):
                w = first_ref[a, b, e]
                v1[(a * 3 + b) * 3 + e] = lax.dot_general(w, grow, tn, preferred_element_type=F32)
            v2[a * 3 + b] = jnp.dot(last_ref[a, b], grow, preferred_element_type=F32)
    m = iota((32, 256), 1) % 32
    li = iota((32, 256), 0)
    masks = [(li == m + a) & (m < STEP + 2) for a in range(3)]

    def first(b, c):
        for e in range(3):
            for i in range(G):
                block = jnp.zeros((32, 256), F32)
                for a in range(3):
                    row = v1[a * 9 + e + 3 * b, i : i + 1, :]
                    block = jnp.where(masks[a], row, block)
                at = (e * G + i) * 32
                t1[0, b, at : at + 32, :] = block.astype(BF16)
        return c

    lax.fori_loop(0, 3, first, 0)
    rows2 = [(m == li + a) & (li < STEP) for a in range(3)]

    def last(b, c):
        for e in range(3):
            block = jnp.zeros((32, 256), F32)
            for a in range(3):
                row = v2[a * 3 + b, e : e + 1, :]
                block = jnp.where(rows2[a], row, block)
            t2[b, e * 32 : e * 32 + 32, :] = block.astype(BF16)
        return c

    lax.fori_loop(0, 3, last, 0)

    lane = iota((W, W), 1)
    w = iota((W, W), 0)
    for p, (ka, kb, turn) in enumerate(PAIRS):
        for n, (k, base) in enumerate(((ka, 0), (kb, 16 * turn))):
            s = (lane + w + 1 - base) & (W - 1)
            ok = (s < 12 * k) & (s <= w)
            band[p, n] = jnp.where(ok, 1.0, 0.0).astype(BF16)
    for gq in range(4):
        low = lane % 32
        d = STEP * ((lane // 32 - gq + 4) % 4) - 2 + low
        real = (low < STEP + 4) & (d >= 0) & (d < D)
        for p, (ka, kb, turn) in enumerate(PAIRS):
            hit = (w == (((d * ka) >> 3) + W - 1) % W) | (w == (((d * kb) >> 3) + 16 * turn - 1) % W)
            pick[gq, p * W : (p + 1) * W, :] = jnp.where(hit & real, 1.0, 0.0).astype(BF16)
    back[...] = jnp.where(lane + w == W - 1, 1.0, 0.0).astype(BF16)

    def turned(b, c):
        for j in range(1, TILES):
            for e in range(3):
                for h in range(2):
                    for q in range(4):
                        at = e * 256 + h * W
                        t1[j, b, at + q * 32 : at + q * 32 + 32, :] = t1[
                            0, b, at + ((q - j) % 4) * 32 : at + ((q - j) % 4) * 32 + 32, :
                        ]
        return c

    lax.fori_loop(0, 3, turned, 0)


def count_points(pts, slot, row, begin, count):
    n = pts.shape[3]
    one = jnp.ones((), BF16)
    zero = jnp.zeros((), BF16)
    bins = iota((104, n), 0)
    spots = iota((256, n), 0).astype(BF16)

    def points(src, totals):
        both = [pts[src, c].astype(F32) for c in range(3)]
        p = [jnp.where(slot == 0, x[0:1], x[1:2]) for x in both]
        left = jnp.where((bins.astype(BF16) == p[2].astype(BF16)) | (bins >= D), one, zero)
        added = []
        for half in range(2):
            local = p[0] - (4 * (row // 2) + 2 * half).astype(F32)
            inside = (local >= 0) & (local < 2)
            code = jnp.where(inside, local * W + p[1], -1.0).astype(BF16)
            right = jnp.where(spots == code, one, zero)
            added.append(
                totals[half] + lax.dot_general(left, right, NT, preferred_element_type=F32)
            )
        return tuple(added)

    nothing = jnp.zeros((104, 256), F32)
    return lax.fori_loop(begin, begin + count, points, (nothing, nothing), unroll=2)


def build_queries(core, win0, qm):
    lane = iota((W, W), 1)

    def one(ro, c):
        rr = ro + 2
        q = win0[rr // 2, core, rr % 2]
        for g in range(G):
            qm[ro, g * W : (g + 1) * W, :] = jnp.where(lane // 16 == g, q, jnp.zeros_like(q))
        return c

    lax.fori_loop(0, NROWS, one, 0)


def score(slot, p, frame, row, shift, win, band, back, qm, kbuf, skew):
    t = 2 * frame + slot
    ka, kb, turn = PAIRS[p]

    def one(ro, c):
        for n, k in enumerate((ka, kb)):
            j = (k - slot + 1) // 2
            fi = slot - k + 2 * j
            rs = ro + 2 + shift[k - 1, t]
            src = 4 * (row // 2) - 4 + rs
            ok = (t - k >= 0) & (src >= 0) & (src < 32)
            key = win[j][rs // 2, fi, rs % 2]
            key = jnp.where(ok, key, jnp.zeros_like(key))
            key = jnp.dot(back[...], key, preferred_element_type=F32).astype(BF16)
            if n:
                cut = W - 16 * turn
                kbuf[ro, W + 16 * turn : 2 * W, :] = key[0:cut]
                kbuf[ro, W : W + 16 * turn, :] = key[cut:W]
            else:
                kbuf[ro, 0:W, :] = key
        m = lax.dot_general(qm[ro], kbuf[ro], NT, preferred_element_type=F32)
        for g in range(G):
            rows = m[g * W : (g + 1) * W].astype(BF16)
            both = rows[:, 0:W] * band[p, 0] + rows[:, W : 2 * W] * band[p, 1]
            skew[ro, g * W : (g + 1) * W, p * W : (p + 1) * W] = pltpu.roll(
                both, 0, 1, stride=1, stride_axis=0
            )
        return c

    lax.fori_loop(0, NROWS, one, 0, unroll=True)


def finish(row, tgt, occ, grad, t1, t2, pick, skew, pad, x3, hid):
    lane = iota((W, W), 1)
    top = 4 * (row // 2)

    def cost_row(ro, c):
        src = top - 2 + ro
        live = (src >= 0) & (src < 32)
        for h in range(2):
            picked = [
                jnp.dot(
                    skew[ro, (4 * h + gq) * W : (4 * h + gq + 1) * W, :],
                    pick[gq],
                    preferred_element_type=F32,
                )
                for gq in range(4)
            ]
            for j in range(TILES):
                x = picked[0]
                for gq in range(1, 4):
                    x = jnp.where(lane // 32 == (j + gq) % 4, picked[gq], x)
                s = 2 * j + h
                pad[s, 8 : 8 + W, :] = jnp.where(live, x * SCALE, 0.0)
                for e in range(3):
                    at = e * 256 + h * W
                    x3[j, ro, :, at : at + W] = pad[s, 7 + e : 7 + e + W, :].astype(BF16)
        return c

    lax.fori_loop(0, NROWS, cost_row, 0, unroll=True)

    def tile(j, c):
        total = jnp.dot(x3[j, 0:6].reshape(6 * W, 768), t1[j, 0], preferred_element_type=F32)
        for b in (1, 2):
            total += jnp.dot(x3[j, b : b + 6].reshape(6 * W, 768), t1[j, b], preferred_element_type=F32)
        d = STEP * j - 1 + iota((W, 256), 1) % 32
        inside = (d >= 0) & (d < D)
        for h in range(6):
            src = top - 1 + h
            ok = inside & ((src >= 0) & (src < 32))
            hid[h] = jnp.where(ok, jnp.maximum(total[h * W : (h + 1) * W], 0.0), 0.0).astype(BF16)
        out = lax.dot_general(
            t2[...].reshape(288, 256), hid[...].reshape(6 * W, 256), NT, preferred_element_type=F32
        )
        for r in range(4):
            cut = (
                out[0:96, r * W : (r + 1) * W]
                + out[96:192, (r + 1) * W : (r + 2) * W]
                + out[192:288, (r + 2) * W : (r + 3) * W]
            )
            wl = iota((STEP, W), 1)
            logits = (
                cut[32 : 32 + STEP]
                + jnp.where(wl == 0, 0.0, pltpu.roll(cut[0:STEP], 1, 1))
                + jnp.where(wl == W - 1, 0.0, pltpu.roll(cut[64 : 64 + STEP], W - 1, 1))
            )
            sig = jax.nn.sigmoid(logits)
            ds = pl.ds(j * STEP, STEP)
            occ[r // 2, ds, r % 2, :] = sig.astype(BF16)
            hits = tgt[D : D + 1, r * W : (r + 1) * W]
            spots = tgt[pl.ds(pl.multiple_of(j * STEP, 8), STEP), r * W : (r + 1) * W]
            grad[r // 2, ds, r % 2, :] = hits * sig - spots
        return c

    lax.fori_loop(0, TILES, tile, 0)


MESH = pl.DeviceIdType.MESH
REACH = 4
ORDER = (0, 1, 4, 3, 2)
EDGE = (1, 3, 4)


def fused_kernel(*refs):
    feat, pts, shift, first_ref, last_ref, occ, grad = refs[:7]
    win = refs[7 : 8 + REACH]
    rest = refs[8 + REACH :]
    allpts, detour, v1, v2, t1, t2, band, pick, back, qm, kbuf, skew, pad, x3, hid, tgt = rest[:16]
    occ_out, grad_out, send, recv, relay_send, psend, precv, own, esend, osend, orecv, dsem = rest[16:]
    f = lax.axis_index("frame")
    r = lax.axis_index("row")
    frames = lax.axis_size("frame")
    rows = lax.axis_size("row")
    core = r % 2
    sibling = r + 1 - 2 * core
    center = 2 + core

    def inside(there):
        return (there >= 0) & (there < rows)

    def crosses(off):
        return inside(r + off) & ((r + off) // (rows // 2) != r // (rows // 2))

    mid = frames // 2

    def by_frames(j, there, off):
        near = (there - j) // mid == there // mid
        edge = {1: near, 3: near | (there == mid), 4: True}.get(j, False)
        inner = {4: (there == mid) | (there == mid + 1), 3: (there == frames - 1) | (there == mid - 1)}.get(j, False)
        return (crosses(off) & edge) | (jnp.logical_not(crosses(off)) & inner)

    barrier = pltpu.get_barrier_semaphore()

    def greet(there_f, there_r):
        pl.semaphore_signal(
            barrier, inc=1, device_id={"frame": there_f, "row": there_r}, device_id_type=MESH
        )

    for off in range(2, rows, 2):
        greet(f, (r + off) % rows)
    greet(f, sibling)
    for j in range(1, REACH + 1):
        pl.when(f + j < frames)(lambda j=j: greet(f + j, r))
        pl.when(f - j >= 0)(lambda j=j: greet(f - j, r))
    later = jnp.minimum(frames - 1 - f, REACH)
    earlier = jnp.minimum(f, REACH)
    pl.semaphore_wait(barrier, rows // 2 + later + earlier)

    def frame_copy(j, there):
        return pltpu.make_async_remote_copy(
            src_ref=feat,
            dst_ref=win[j].at[center],
            send_sem=send.at[0, j],
            recv_sem=recv.at[center, j],
            device_id={"frame": there, "row": r},
            device_id_type=MESH,
        )

    def detour_copy():
        return pltpu.make_async_remote_copy(
            src_ref=feat,
            dst_ref=detour,
            send_sem=dsem.at[0],
            recv_sem=dsem.at[1],
            device_id={"frame": 0, "row": r},
            device_id_type=MESH,
        )

    def onward_copy():
        return pltpu.make_async_remote_copy(
            src_ref=detour,
            dst_ref=win[1].at[center],
            send_sem=dsem.at[2],
            recv_sem=recv.at[center, 1],
            device_id={"frame": mid, "row": r},
            device_id_type=MESH,
        )

    def direct(j):
        return (f + j < frames) & ((j != 1) | (f != mid - 1))

    def row_copy(lane, j, q, there):
        return pltpu.make_async_remote_copy(
            src_ref=feat if j == 0 else win[j].at[center],
            dst_ref=win[j].at[q],
            send_sem=send.at[lane, j],
            recv_sem=recv.at[q, j],
            device_id={"frame": f, "row": there},
            device_id_type=MESH,
        )

    def relay_copy(n, j, q):
        return pltpu.make_async_remote_copy(
            src_ref=win[j].at[q],
            dst_ref=win[j].at[q],
            send_sem=relay_send.at[n, j],
            recv_sem=recv.at[q, j],
            device_id={"frame": f, "row": sibling},
            device_id_type=MESH,
        )

    def point_copy(n, src, slot, there):
        return pltpu.make_async_remote_copy(
            src_ref=src,
            dst_ref=allpts.at[slot],
            send_sem=psend.at[n],
            recv_sem=precv.at[slot],
            device_id={"frame": f, "row": there},
            device_id_type=MESH,
        )

    def points_out(act):
        act(point_copy(1, pts, r, sibling))
        for off in range(2, rows, 2):
            act(point_copy(off, pts, r, (r + off) % rows))

    def points_on(act, wait_first):
        for off in range(2, rows, 2):
            there = (r + off) % rows
            if wait_first:
                point_copy(off, pts, there, sibling).wait_recv()
            act(point_copy(off + 1, allpts.at[there], there, sibling))

    def row_sends(j, act):
        for lane, q, off in ((2, core, 2), (3, 4 + core, -2)):
            ok = inside(r + off) & (f >= j)
            if j in EDGE:
                ok = ok & jnp.logical_not(by_frames(j, f, off))
            pl.when(ok)(lambda lane=lane, q=q, off=off: act(row_copy(lane, j, q, r + off)))
        pl.when(f >= j)(lambda: act(row_copy(1, j, center, sibling)))

    def edge_sends(act):
        for n, (q, off) in enumerate(((core, -2), (4 + core, 2))):
            for j in EDGE:
                copy = pltpu.make_async_remote_copy(
                    src_ref=win[0].at[q],
                    dst_ref=win[j].at[q],
                    send_sem=esend.at[n, j],
                    recv_sem=recv.at[q, j],
                    device_id={"frame": f + j, "row": r},
                    device_id_type=MESH,
                )
                ok = inside(r + off) & (f + j < frames) & by_frames(j, f + j, off)
                pl.when(ok)(lambda copy=copy: act(copy))

    def relay(j, act, wait_first):
        for n, (q, off) in enumerate(((core, -2), (4 + core, 2))):

            def body(n=n, q=q):
                copy = relay_copy(n, j, q)
                if wait_first:
                    copy.wait_recv()
                act(copy)

            pl.when(inside(r + off) & (f >= j))(body)

    def start(copy):
        copy.start()

    def arrive(j):
        pl.when(f >= j)(lambda: row_copy(1, j, 5 - center, sibling).wait_recv())
        for q, off in ((1 - core, -2), (5 - core, 2)):
            ok = inside(r + off) & (f >= j)
            pl.when(ok)(lambda q=q: row_copy(1, j, q, sibling).wait_recv())

    def step(j):
        pl.when(f >= j)(lambda: frame_copy(j, f).wait_recv())
        row_sends(j, start)

    def count(part):
        counts = count_points(allpts, core, r, part * (rows // 4), rows // 4)
        for half in range(2):
            tgt[:, half * 256 : half * 256 + 256] += counts[half]

    def scores(slot, p):
        score(slot, p, f, r, shift, win, band, back, qm, kbuf, skew)

    mine = pltpu.make_async_copy(feat, win[0].at[center], own.at[0])
    mine_pts = pltpu.make_async_copy(pts, allpts.at[r], own.at[1])
    points_out(start)
    mine.start()
    mine_pts.start()
    row_sends(0, start)
    pl.when(f == mid - 1)(lambda: detour_copy().start())
    for j in (1, 4, 3, 2):
        pl.when(direct(j))(lambda j=j: frame_copy(j, f + j).start())

    @pl.when(f == 0)
    def _():
        detour_copy().wait_recv()
        onward_copy().start()

    build_tables(first_ref, last_ref, v1, v2, t1, t2, band, pick, back)
    for s in range(2 * TILES):
        pad[s, 0:8, :] = jnp.zeros((8, W), F32)
        pad[s, 136:144, :] = jnp.zeros((8, W), F32)
    tgt[...] = jnp.zeros_like(tgt)
    step(1)
    step(4)
    points_on(start, True)
    relay(0, start, True)
    edge_sends(start)
    point_copy(1, pts, sibling, sibling).wait_recv()
    for off in range(2, rows, 2):
        point_copy(off, pts, (sibling + off) % rows, sibling).wait_recv()
    mine.wait()
    mine_pts.wait()
    count(0)
    step(3)
    step(2)
    relay(1, start, True)
    count(1)
    relay(4, start, True)
    count(2)
    arrive(0)
    build_queries(core, win[0], qm)
    relay(3, start, True)
    count(3)
    arrive(1)
    arrive(4)

    @pl.when(core == 0)
    def _():
        scores(0, 0)
        scores(0, 1)

    @pl.when(core == 1)
    def _():
        scores(1, 0)

    relay(2, start, True)
    arrive(3)

    @pl.when(core == 1)
    def _():
        scores(1, 1)
        scores(1, 2)

    arrive(2)

    @pl.when(core == 0)
    def _():
        scores(0, 2)
        scores(0, 3)

    @pl.when(core == 1)
    def _():
        scores(1, 3)

    finish(r, tgt, occ_out, grad_out, t1, t2, pick, skew, pad, x3, hid)

    def swap(n, src, dst):
        return pltpu.make_async_remote_copy(
            src_ref=src.at[1 - core],
            dst_ref=dst.at[core],
            send_sem=osend.at[n],
            recv_sem=orecv.at[n],
            device_id={"frame": f, "row": sibling},
            device_id_type=MESH,
        )

    swaps = (swap(0, occ_out, occ), swap(1, grad_out, grad))
    keeps = (
        pltpu.make_async_copy(occ_out.at[core], occ.at[core], own.at[2]),
        pltpu.make_async_copy(grad_out.at[core], grad.at[core], own.at[3]),
    )
    for copy in swaps + keeps:
        copy.start()
    for j in range(1, REACH + 1):
        pl.when(direct(j))(lambda j=j: frame_copy(j, f + j).wait_send())
    pl.when(f == mid - 1)(lambda: detour_copy().wait_send())
    pl.when(f == 0)(lambda: onward_copy().wait_send())
    edge_sends(lambda copy: copy.wait_send())
    for j in ORDER:
        row_sends(j, lambda copy: copy.wait_send())
        relay(j, lambda copy: copy.wait_send(), False)
    points_out(lambda copy: copy.wait_send())
    points_on(lambda copy: copy.wait_send(), False)
    for copy in swaps + keeps:
        copy.wait()


def settle_kernel(occ, grad, occ_out, grad_out):
    occ_out[...] = occ[...]
    grad_out[...] = grad[...]


def settle(occ, grad):
    block = pl.BlockSpec((1, D, 2, W), lambda s: (s, 0, 0, 0))
    return pl.pallas_call(
        settle_kernel,
        grid=(2,),
        out_shape=(
            jax.ShapeDtypeStruct(occ.shape, occ.dtype),
            jax.ShapeDtypeStruct(grad.shape, grad.dtype),
        ),
        in_specs=[block, block],
        out_specs=(block, block),
        name="settle",
    )(occ, grad)


def shards(features, row_shift, lidar_points, conv_first, conv_last):
    points = jnp.transpose(lidar_points, (1, 0, 2))
    first = jnp.transpose(conv_first, (2, 3, 4, 0, 1))
    last = jnp.transpose(conv_last[0], (1, 2, 3, 0))
    count = lax.axis_size("row")
    vmem = pl.BlockSpec(memory_space=pltpu.VMEM)
    smem = pl.BlockSpec(memory_space=pltpu.SMEM)
    hbm = pl.BlockSpec(memory_space=pl.ANY)
    dma = pltpu.SemaphoreType.DMA
    both = pl.pallas_call(
        fused_kernel,
        out_shape=(
            jax.ShapeDtypeStruct((2, D, 2, W), BF16),
            jax.ShapeDtypeStruct((2, D, 2, W), F32),
        ),
        in_specs=[vmem, vmem, smem, vmem, vmem],
        out_specs=(hbm, hbm),
        scratch_shapes=[pltpu.VMEM((6,) + features.shape, BF16) for _ in range(REACH + 1)]
        + [
            pltpu.VMEM((count,) + points.shape, I32),
            pltpu.VMEM(features.shape, BF16),
            pltpu.VMEM((27, G, 256), F32),
            pltpu.VMEM((9, 3, 256), F32),
            pltpu.VMEM((TILES, 3, 768, 256), BF16),
            pltpu.VMEM((3, 96, 256), BF16),
            pltpu.VMEM((4, 2, W, W), BF16),
            pltpu.VMEM((4, 4 * W, W), BF16),
            pltpu.VMEM((W, W), BF16),
            pltpu.VMEM((NROWS, G * W, W), BF16),
            pltpu.VMEM((NROWS, 2 * W, W), BF16),
            pltpu.VMEM((NROWS, G * W, 4 * W), BF16),
            pltpu.VMEM((2 * TILES, 144, W), F32),
            pltpu.VMEM((TILES, NROWS, W, 768), BF16),
            pltpu.VMEM((6, W, 256), BF16),
            pltpu.VMEM((104, 512), F32),
            pltpu.VMEM((2, D, 2, W), BF16),
            pltpu.VMEM((2, D, 2, W), F32),
            dma((4, REACH + 1)),
            dma((6, REACH + 1)),
            dma((2, REACH + 1)),
            dma((count,)),
            dma((count,)),
            dma((4,)),
            dma((2, REACH + 1)),
            dma((2,)),
            dma((2,)),
            dma((3,)),
        ],
        compiler_params=pltpu.CompilerParams(
            collective_id=0, has_side_effects=True, vmem_limit_bytes=60000 * 1024
        ),
        name="fused_volume",
    )(features, points, row_shift.T, first, last)
    return settle(*both)


def solution(mesh):
    P = jax.sharding.PartitionSpec
    out = P("frame", None, "row", None)
    return jax.shard_map(
        shards,
        mesh=mesh,
        in_specs=(P("frame", "row", None, None), P(), P("frame", None, "row"), P(), P()),
        out_specs=(out, out),
        check_vma=False,
    )
```
